128 devices in a mesh: row: 8 (over y, z_hi), col: 16 (over x, z_lo, core).
Axes of the slice: x: 4, y: 4, z: 4 (z_hi: 2, z_lo: 2; z = z_hi * 2 + z_lo), core: 2. Of those that a mesh axis runs over, the one named last changes fastest.
Arguments:
- band_factors: bfloat16 [48, 48, 8, 256], P('col'), may hold values from -6 to 6
- pair_density: bfloat16 [48, 48, 16, 256], P('col'), may hold values from -6 to 6
- screened: bfloat16 [48, 48, 256, 256], P('col'), may hold values from -1 to 3, as said below
- coulomb: float32 [256], replicated, may hold values from 0.2 to 2
- window_mask: int32 [3, 48, 48], P(None, 'row'), may hold values 0 or 1
- trial_vector: bfloat16 [16, 48, 48], P(None, 'col'), may hold values from -0.0013809204 to 0.0013809204
Outputs:
- row_image: float32 [16, 3, 48], P('col', None, 'row')
- col_image: float32 [16, 48, 48], P(None, 'col', 'row')
The draws below stay inside these ranges and needn't reach their ends.
Inputs may be any that keep to these rules, and one draw needn't show every extreme that they name: `screened`: every block is symmetric.
All inputs are finite; a program needn't handle non-finite values. No bound on the sum of `window_mask` on one device may be relied on, other than what follows from the above.
Results may differ from the reference program's by a relative error of at most 0.0041.
Values may be sent and summed in bfloat16 or wider, within the bound.
A program may use at most 192 MiB of HBM per device.

```python
import math
import jax
import jax.numpy as jnp
from jax import lax

G = 256
BANDS = 8
PAIRS = 16
MESH = 48
CR = 3
NK = 2304
N_COL = 16


def draw_screened(key, part):
    first_key, second_key = jax.random.split(jax.random.fold_in(key, 11))
    base = jax.random.normal(first_key, (MESH, MESH, G, G), jnp.float32)
    symmetric = (base + jnp.swapaxes(base, 2, 3)) * (0.5 / math.sqrt(G))
    diagonal = jnp.exp(jax.random.uniform(second_key, (MESH, MESH, G), jnp.float32, -0.7, 0.7))
    return (symmetric + diagonal[..., None] * jnp.eye(G, dtype=jnp.float32)).astype(jnp.bfloat16)


def plant(drawn, rng, smallest, top_value):
    longest = drawn.shape.index(max(drawn.shape))
    spots = []
    for shift in (0, 1):
        where = [jax.random.randint(jax.random.fold_in(rng, axis), (), 0, length) for axis, length in enumerate(drawn.shape)]
        where[longest] = (where[longest] + shift) % drawn.shape[longest]
        spots.append(tuple(where))
    return drawn.at[spots[0]].set(smallest).at[spots[1]].set(top_value)


def block_levels(own_key, dims, cuts, smallest, high):
    def one(position, parts):
        heights = jax.random.uniform(jax.random.fold_in(jax.random.fold_in(own_key, 6), position), (parts,), jnp.float32, smallest / len(cuts), high / len(cuts))
        return jnp.repeat(jnp.exp(heights), dims[position] // parts).reshape((-1,) + (1,) * (len(dims) - position - 1))

    level = one(*cuts[0])
    for cut in cuts[1:]:
        level = level * one(*cut)
    return level


def scatter_about(stream_key, extent, width, most, cuts=(), kind=jnp.bfloat16):
    result = width * jax.random.normal(stream_key, extent, jnp.float32)
    if cuts:
        result = result * block_levels(stream_key, extent, cuts, -0.22, 0.18)
    return jnp.clip(result, -most, most).astype(kind)


def setup_inputs(seed: int = 0) -> dict:
    streams_of = jax.random.split(jax.random.key(seed), 7)
    return {
        "band_factors": scatter_about(streams_of[0], (MESH, MESH, BANDS, G), 1.0, 6.0, ((0, 16),)),
        "pair_density": scatter_about(streams_of[1], (MESH, MESH, PAIRS, G), 1.0, 6.0, ((0, 16),)),
        "screened": draw_screened(jax.random.fold_in(streams_of[6], 71), 0),
        "coulomb": jnp.clip(jnp.exp(jax.random.uniform(streams_of[3], (G,), jnp.float32, math.log(0.2), math.log(2.0))), 0.2, 2.0),
        "window_mask": plant((jax.random.randint(streams_of[4], (CR, MESH, MESH), 0, 4) < 3).astype(jnp.int32), jax.random.fold_in(streams_of[4], 1), 0, 1),
        "trial_vector": scatter_about(streams_of[5], (PAIRS, MESH, MESH), ((2 * NK * PAIRS * G) ** -0.5), 0.0013809204, ((1, 16),)),
    }


HIGHEST_PRECISION = lax.Precision.HIGHEST


def pair_block(row_bands, row_pairs, row_trial, row_line, col_bands, col_pairs, col_trial, col_line, w_row, coulomb, mask_line):
    mesh_side = row_bands.shape[0]
    band_half = row_bands.shape[1] // 2
    fourier = row_bands.shape[2]
    offsets = jnp.arange(mesh_side, dtype=jnp.int32)
    places = (offsets[None, :] + offsets[:, None]) % mesh_side
    chosen_bands = jnp.take(col_bands, places, axis=0).astype(jnp.float32)
    chosen_pairs = jnp.take(col_pairs, places, axis=0).astype(jnp.float32)
    own_bands = row_bands.astype(jnp.float32)
    left_pair = (own_bands[None, :, :band_half, None, :] * chosen_bands[:, :, None, :band_half, :]).astype(jnp.bfloat16)
    right_pair = (own_bands[None, :, band_half:, None, :] * chosen_bands[:, :, None, band_half:, :]).astype(jnp.bfloat16)
    mixed_pair = jnp.einsum("qng,qgh->qnh", left_pair.reshape(mesh_side, -1, fourier).astype(jnp.float32), w_row.astype(jnp.float32)).astype(jnp.bfloat16)
    mixed_pair = mixed_pair.reshape(mesh_side, mesh_side, band_half, band_half, fourier)
    direct = jnp.einsum("qbach,qbvwh->qbvawc", mixed_pair.astype(jnp.float32), right_pair.astype(jnp.float32))
    direct = direct.reshape(mesh_side, mesh_side, band_half * band_half, band_half * band_half)
    scaled = (row_pairs.astype(jnp.float32) * coulomb).astype(jnp.bfloat16)
    exchange_term = jnp.einsum("bsg,qbug->qbsu", scaled.astype(jnp.float32), chosen_pairs)
    kernel = 2.0 * exchange_term - direct
    row_place = row_line * mesh_side + offsets
    col_place = col_line * mesh_side + places
    kept = (col_place >= row_place[None, :]) & (mask_line[None, :] > 0)
    kernel = jnp.where(kept[..., None, None], kernel, jnp.float32(0.0))
    col_values = jnp.take(col_trial.astype(jnp.float32), places, axis=1)
    row_part = jnp.einsum("qbsu,uqb->sb", kernel, col_values, precision=HIGHEST_PRECISION)
    strict = col_place > row_place[None, :]
    col_each = jnp.einsum("qbsu,sb->uqb", jnp.where(strict[..., None, None], kernel, jnp.float32(0.0)), row_trial.astype(jnp.float32), precision=HIGHEST_PRECISION)
    onehot = (places[:, :, None] == offsets[None, None, :]).astype(jnp.float32)
    col_part = jnp.einsum("uqb,qbc->uc", col_each, onehot, precision=HIGHEST_PRECISION)
    return row_part, col_part


def reference(band_factors, pair_density, screened, coulomb, window_mask, trial_vector):
    mesh_side = MESH
    first_line = MESH // 2
    band_lines = MESH // N_COL
    upper_lines = mesh_side - first_line
    row_lines = jnp.repeat(jnp.arange(band_lines, dtype=jnp.int32), upper_lines)
    col_lines = jnp.tile(first_line + jnp.arange(upper_lines, dtype=jnp.int32), band_lines)

    def per_pair(indices):
        panel_line, col_line = indices
        row_line = first_line + panel_line
        shift_line = (col_line - row_line) % mesh_side
        return pair_block(band_factors[row_line], pair_density[row_line], trial_vector[:, row_line], row_line, band_factors[col_line], pair_density[col_line], trial_vector[:, col_line], col_line, screened[shift_line], coulomb, window_mask[panel_line, :, col_line])

    row_parts, col_parts = lax.map(per_pair, (row_lines, col_lines))
    row_image = row_parts.reshape(band_lines, upper_lines, PAIRS, mesh_side).sum(axis=1).transpose(1, 0, 2)
    col_upper = col_parts.reshape(band_lines, upper_lines, PAIRS, mesh_side).sum(axis=0).transpose(1, 0, 2)
    col_image = jnp.concatenate([jnp.zeros((PAIRS, first_line, mesh_side), jnp.float32), col_upper], axis=1)
    return row_image, col_image
```

```python
import functools

import jax
import jax.numpy as jnp
from jax import lax
from jax.experimental import pallas as pl
from jax.experimental.pallas import tpu as pltpu
from jax.sharding import PartitionSpec as P

MESH = pl.DeviceIdType.MESH
F32 = jnp.float32
BF16 = jnp.bfloat16
SIDE = 48
ROWS = 8
WIDTH = 6
LINES = 3
HALF = 8
SLOTS = 2 * LINES - 1
RING = SIDE + 8
Q_STEP = 4
HIGHEST = lax.Precision.HIGHEST
ANY = pl.BlockSpec(memory_space=pl.ANY)
VMEM = pl.BlockSpec(memory_space=pltpu.VMEM)


def iota(shape, axis):
    return lax.broadcasted_iota(jnp.int32, shape, axis)


def dot(a, b, contract=(1, 0), precision=None):
    return lax.dot_general(
        a,
        b,
        (((contract[0],), (contract[1],)), ((), ())),
        preferred_element_type=F32,
        precision=precision,
    )


def ones_where(condition, dtype=BF16):
    return jnp.where(condition, 1.0, 0.0).astype(dtype)


def block_diagonal(trial_line, first, copies):
    pick = ones_where(iota((8, SIDE), 1) == first + iota((8, SIDE), 0))
    rows = dot(pick, trial_line).astype(BF16)
    tiled = dot(rows, ones_where(iota((16, copies * 16), 1) % 16 == iota((16, copies * 16), 0)))
    return jnp.where(iota(tiled.shape, 1) // 16 == iota(tiled.shape, 0), tiled, 0.0)


def greet():
    row, col = lax.axis_index("row"), lax.axis_index("col")
    barrier = pltpu.get_barrier_semaphore()
    for step in range(1, ROWS):
        pl.semaphore_signal(
            barrier, inc=1, device_id=(lax.rem(row + step, ROWS), col), device_id_type=MESH
        )
    for step in range(1, 2 * HALF):
        pl.semaphore_signal(
            barrier, inc=1, device_id=(row, lax.rem(col + step, 2 * HALF)), device_id_type=MESH
        )
    pl.semaphore_wait(barrier, ROWS + 2 * HALF - 2)


def remote(source, target, send_sem, recv_sem, device):
    return pltpu.make_async_remote_copy(
        src_ref=source,
        dst_ref=target,
        send_sem=send_sem,
        recv_sem=recv_sem,
        device_id=device,
        device_id_type=MESH,
    )


def gather_kernel(
    bands,
    density,
    trial,
    window,
    trial_v,
    coulomb,
    panel,
    masks,
    cols,
    ctrial,
    ptrial,
    rvec,
    dens_v,
    rsend,
    send,
    recv,
    local,
):
    row, col = lax.axis_index("row"), lax.axis_index("col")
    first = row * WIDTH
    greet()
    own = bands.at[:, pl.ds(first, WIDTH)]

    def to(source, target, number, arrives, device):
        return remote(source, target, send.at[number], recv.at[arrives], device)

    def column_copies():
        near = (row, lax.rem(col + HALF, 2 * HALF))
        return [
            to(own, cols.at[0:LINES], 8, 0, near),
            to(trial, ctrial.at[0], 9, 2, near),
        ]

    def next_copies():
        far = (row, lax.rem(col + HALF - 1, 2 * HALF))
        return [
            to(bands.at[0 : LINES - 1, pl.ds(first, WIDTH)], cols.at[LINES:SLOTS], 10, 1, far),
            to(trial, ctrial.at[1], 11, 3, far),
        ]

    def panel_copies():
        return [to(own, panel.at[row], j, 5, (row, j)) for j in range(HALF)] + [
            to(trial, ptrial, 16 + j, 4, (row, j)) for j in range(HALF)
        ]

    def vector_copies():
        return [to(rsend, rvec, 24 + j, 6, (row, HALF + j)) for j in range(1, HALF)]

    def row_copies():
        copies = []
        for step in range(1, ROWS):
            peer = lax.rem(row + step, ROWS)
            copies.append(to(panel.at[row], panel.at[row], step, 8 + step, (peer, col)))
        return copies

    def mask_copies():
        copies = []
        for step in range(1, ROWS):
            peer = lax.rem(row + step, ROWS)
            copies.append(to(window, masks.at[row], 8 + step, 16 + step, (peer, col)))
        return copies

    @pl.when(col < HALF)
    def _():
        keep = pltpu.make_async_copy(window, masks.at[row], local.at[0])
        keep.start()
        for copy in mask_copies():
            copy.start()
        to(own, panel.at[row], 0, 5, (row, HALF)).wait_recv()
        for copy in row_copies():
            copy.start()
        to(own, cols.at[0:LINES], 0, 0, (row, HALF)).wait_recv()
        to(trial, ctrial.at[0], 0, 2, (row, HALF)).wait_recv()
        to(trial, ptrial, 0, 4, (row, HALF)).wait_recv()

        @pl.when(col < HALF - 1)
        def _():
            to(cols.at[LINES:SLOTS], cols.at[LINES:SLOTS], 0, 1, (row, HALF)).wait_recv()
            to(trial, ctrial.at[1], 0, 3, (row, HALF)).wait_recv()

        for step in range(1, ROWS):
            source = lax.rem(row + ROWS - step, ROWS)
            to(panel.at[source], panel.at[source], 0, 8 + step, (source, col)).wait_recv()
            to(window, masks.at[source], 0, 16 + step, (source, col)).wait_recv()
        for copy in row_copies():
            copy.wait_send()
        for copy in mask_copies():
            copy.wait_send()
        keep.wait()

    @pl.when(col >= HALF)
    def _():
        @pl.when(col == HALF)
        def _():
            fetch = pltpu.make_async_copy(density.at[:, pl.ds(first, WIDTH)], dens_v, local.at[0])
            fetch.start()
            for copy in panel_copies():
                copy.start()
            fetch.wait()
            for t in range(LINES):
                diagonal = block_diagonal(trial_v[t], first, WIDTH).astype(BF16)
                scaled = (dens_v[t].astype(F32) * coulomb[...]).astype(BF16)
                rsend[t] = dot(diagonal, scaled.reshape(WIDTH * 16, 256))
            for copy in vector_copies():
                copy.start()
            keep = pltpu.make_async_copy(rsend, rvec, local.at[1])
            keep.start()
            keep.wait()

        for copy in column_copies():
            copy.start()

        @pl.when(col > HALF)
        def _():
            for copy in next_copies():
                copy.start()
            to(rsend, rvec, 0, 6, (row, HALF)).wait_recv()
            for copy in next_copies():
                copy.wait_send()

        for copy in column_copies():
            copy.wait_send()

        @pl.when(col == HALF)
        def _():
            for copy in panel_copies():
                copy.wait_send()
            for copy in vector_copies():
                copy.wait_send()


def gather(bands, density, trial, window, coulomb):
    shapes = [
        jax.ShapeDtypeStruct((ROWS, LINES, WIDTH, 8, 256), BF16),
        jax.ShapeDtypeStruct((ROWS, LINES, WIDTH, SIDE), jnp.int32),
        jax.ShapeDtypeStruct((SLOTS, WIDTH, 8, 256), BF16),
        jax.ShapeDtypeStruct((2, LINES, SIDE, 16), BF16),
        jax.ShapeDtypeStruct((LINES, SIDE, 16), BF16),
        jax.ShapeDtypeStruct((LINES, 8, 256), F32),
    ]
    return pl.pallas_call(
        gather_kernel,
        name="gather",
        out_shape=shapes,
        in_specs=[ANY, ANY, ANY, ANY, VMEM, VMEM],
        out_specs=[ANY] * len(shapes),
        scratch_shapes=[
            pltpu.VMEM((LINES, WIDTH, 16, 256), BF16),
            pltpu.VMEM((LINES, 8, 256), F32),
            pltpu.SemaphoreType.DMA((32,)),
            pltpu.SemaphoreType.DMA((24,)),
            pltpu.SemaphoreType.DMA((2,)),
        ],
        compiler_params=pltpu.CompilerParams(collective_id=0, has_side_effects=True),
    )(bands, density, trial, window, trial, coulomb)


def pair_kernel(
    blocks,
    panel,
    masks,
    cols,
    ctrial,
    ptrial,
    density,
    rvec,
    trial,
    window,
    zrow,
    zcol,
    pvec,
    zex,
    flat,
    left_t,
    y_row,
    keep_t,
    r_sum,
    col_flat,
    u_col,
    y_col,
    c_sum,
):
    row, col = lax.axis_index("row"), lax.axis_index("col")
    step = pl.program_id(0)
    first = row * WIDTH
    halves = (slice(0, 128), slice(128, 256))
    spread = ones_where(iota((16, 2048), 1) // 128 == iota((16, 2048), 0))

    def lane(expanded, s):
        return expanded[:, s * 128 : (s + 1) * 128]

    def store_ring(table, h, number, value):
        base = number * RING
        table[h, base : base + SIDE, :] = value
        table[h, base + SIDE : base + RING, :] = value[0:8]

    def prepare_panel():
        for t in range(LINES):
            for source in range(ROWS):
                value = panel[source, t].astype(F32).reshape(SIDE, 256)
                base = (t * ROWS + source) * SIDE
                for h in range(2):
                    flat[h, base : base + SIDE, :] = value[:, halves[h]]
        for t in range(LINES):
            expanded = dot(ptrial[t], spread)
            for h in range(2):

                def band(number):
                    return flat[h, pl.ds(t * 8 * SIDE + number, SIDE, stride=8), :]

                for c in range(4):
                    store_ring(left_t, h, t * 4 + c, band(c))
                valence = [band(4 + v) for v in range(4)]
                for c in range(4):
                    total = valence[0] * lane(expanded, c)
                    for v in range(1, 4):
                        total += valence[v] * lane(expanded, 4 * v + c)
                    store_ring(y_row, h, t * 4 + c, total)
        places = iota((WIDTH, SIDE), 1)
        for t in range(LINES):
            for e in range(LINES):
                line = HALF * LINES + t + col * LINES + e
                base = (e * LINES + t) * RING
                for source in range(ROWS):
                    held = jnp.where(places == line, masks[source, t], 0).astype(F32)
                    factor = jnp.broadcast_to(jnp.sum(held, axis=1, keepdims=True), (WIDTH, 128))
                    keep_t[base + source * WIDTH : base + (source + 1) * WIDTH, :] = factor
                keep_t[base + SIDE : base + RING, :] = keep_t[base : base + 8, :]
        r_sum[...] = jnp.zeros_like(r_sum)

    def prepare_columns():
        col_flat[...] = jnp.zeros_like(col_flat)
        for a in range(SLOTS):
            value = cols[a].astype(F32).reshape(WIDTH * 8, 256)
            if a >= LINES:
                value = jnp.where(col < HALF - 1, value, 0.0)
            for h in range(2):
                col_flat[h, a * 64 : a * 64 + WIDTH * 8, :] = value[:, halves[h]]
        pick = ones_where(iota((8, SIDE), 1) == first + iota((8, SIDE), 0))
        for a in range(SLOTS):
            line = ctrial[a // LINES, a % LINES]
            expanded = dot(dot(pick, line).astype(BF16), spread)
            if a >= LINES:
                expanded = jnp.where(col < HALF - 1, expanded, 0.0)
            for h in range(2):

                def band(number):
                    return col_flat[h, pl.ds(a * 64 + number, 8, stride=8), :]

                for pair in range(2):
                    both = jnp.concatenate([band(2 * pair), band(2 * pair + 1)], axis=0)
                    u_col[a * 32 + pair * 16 : a * 32 + pair * 16 + 16, halves[h]] = both.astype(
                        BF16
                    )
                valence = [band(4 + v) for v in range(4)]
                for c in range(4):
                    total = valence[0] * lane(expanded, c)
                    for v in range(1, 4):
                        total += valence[v] * lane(expanded, 4 * v + c)
                    y_col[h, (a * 4 + c) * 8 : (a * 4 + c) * 8 + 8, :] = total
        c_sum[...] = jnp.zeros_like(c_sum)

    def one_block(qq, carry):
        q_value = step * Q_STEP + qq
        start = lax.rem(first + SIDE - q_value, SIDE)
        inside = (first + iota((8, 128), 0) >= q_value) | (col > 0)
        same = (q_value == 0) & (col == 0)
        for t in range(LINES):

            def rows(table, c, h):
                return table[h, pl.ds((t * 4 + c) * RING + start, 8), :]

            lefts = [[rows(left_t, c, h) for h in range(2)] for c in range(4)]
            backs = [[rows(y_row, c, h) for h in range(2)] for c in range(4)]
            totals = [[None, None] for _ in range(4)]
            for e in range(LINES):
                a = t + e
                factor = keep_t[pl.ds((e * LINES + t) * RING + start, 8), :]
                if e == 0:
                    factor = jnp.where(inside, factor, 0.0)
                tiles = []
                for c in range(4):
                    both = []
                    for h in range(2):
                        kept = lefts[c][h] * factor
                        both.append(jnp.concatenate([kept, kept], axis=0).astype(BF16))
                    both = jnp.concatenate(both, axis=1)
                    for pair in range(2):
                        base = a * 32 + pair * 16
                        tiles.append(both * u_col[base : base + 16, :])
                mixed = dot(jnp.concatenate(tiles, axis=0), blocks[e, qq])
                for h in range(2):
                    images = [None] * 4
                    for c in range(4):
                        for d in range(4):
                            base = (c * 4 + d) * 8
                            piece = mixed[base : base + 8, halves[h]]
                            base = (a * 4 + d) * 8
                            part = piece * y_col[h, base : base + 8, :]
                            totals[c][h] = part if totals[c][h] is None else totals[c][h] + part
                            part = piece * backs[c][h]
                            images[d] = part if images[d] is None else images[d] + part
                    for d in range(4):
                        base = (a * 4 + d) * 8
                        image = jnp.where(same, 0.0, images[d]) if e == 0 else images[d]
                        c_sum[h, base : base + 8, :] += image
            for c in range(4):
                for h in range(2):
                    r_sum[h, pl.ds((t * 4 + c) * RING + start, 8), :] += totals[c][h]
        return carry

    def finish():
        lanes = iota((SIDE, 128), 1)
        image = jnp.zeros((SIDE, 128), F32)
        for t in range(LINES):
            for c in range(4):
                base = (t * 4 + c) * RING
                total = []
                for h in range(2):
                    head = r_sum[h, base : base + 8, :] + r_sum[h, base + SIDE : base + RING, :]
                    total.append(
                        jnp.concatenate([head, r_sum[h, base + 8 : base + SIDE, :]], axis=0)
                    )
                for v in range(4):
                    product = 0.0
                    for h in range(2):
                        strided = pl.ds(t * 8 * SIDE + 4 + v, SIDE, stride=8)
                        product += flat[h, strided, :] * total[h]
                    value = jnp.sum(product, axis=1, keepdims=True)
                    image = jnp.where(lanes == t * 16 + 4 * v + c, value, image)
        for target in range(ROWS):
            zrow[target, 0:WIDTH, :] = -image[target * WIDTH : (target + 1) * WIDTH]
            zrow[target, WIDTH:8, :] = jnp.zeros((8 - WIDTH, 128), F32)
        lanes = iota((8, 128), 1)
        for a in range(SLOTS):
            image = jnp.zeros((8, 128), F32)
            for v in range(4):
                for c in range(4):
                    product = 0.0
                    for h in range(2):
                        base = (a * 4 + c) * 8
                        strided = pl.ds(a * 64 + 4 + v, 8, stride=8)
                        product += col_flat[h, strided, :] * c_sum[h, base : base + 8, :]
                    value = jnp.sum(product, axis=1, keepdims=True)
                    image = jnp.where(lanes == 4 * v + c, value, image)
            zcol[a] = -image

    def exchange():
        tile = ones_where(iota((16, SIDE * 16), 1) % 16 == iota((16, SIDE * 16), 0))
        own_point = iota((SIDE, SIDE * 16), 1) // 16 == iota((SIDE, SIDE * 16), 0)
        ones = jnp.ones((8, SIDE), BF16)
        points = iota((8, SIDE * 16), 1) // 16
        row_points = first + iota((8, SIDE * 16), 0)
        places = iota((WIDTH, SIDE), 1)
        wide = jnp.concatenate([rvec[t] for t in range(LINES)], axis=0)
        high = wide.astype(BF16)
        low = (wide - high.astype(F32)).astype(BF16)
        split = jnp.concatenate([high, low], axis=0)
        zex[...] = jnp.zeros_like(zex)
        sums = jnp.zeros((8 * LINES, 256), F32)
        for a in range(LINES):
            line = col * LINES + a
            values = jnp.where(own_point, dot(trial[a], tile), 0.0).astype(BF16)
            values = dot(ones, values)
            kept_values = []
            strict_factors = []
            for t in range(LINES):
                row_line = HALF * LINES + t
                held = jnp.where(places == line, window[t], 0).astype(F32)
                held = jnp.sum(held, axis=1, keepdims=True)
                held = jnp.concatenate([held, jnp.zeros((8 - WIDTH, 1), F32)], axis=0)
                kept = (line > row_line) | ((line == row_line) & (points >= row_points))
                strict = (line > row_line) | ((line == row_line) & (points > row_points))
                kept_values.append(jnp.where(kept, held, 0.0) * values)
                strict_factors.append(jnp.where(strict, held, 0.0))
            table = density[a].reshape(SIDE * 16, 256)
            sums += dot(jnp.concatenate(kept_values, axis=0).astype(BF16), table)
            products = dot(split, table, (1, 1))
            products = products[0 : 8 * LINES] + products[8 * LINES : 16 * LINES]
            image = jnp.sum(
                products * jnp.concatenate(strict_factors, axis=0), axis=0, keepdims=True
            )
            for target in range(ROWS):
                lanes = slice(target * WIDTH * 16, (target + 1) * WIDTH * 16)
                zex[target, a : a + 1, 0 : WIDTH * 16] = 2.0 * image[:, lanes]
        for t in range(LINES):
            pvec[t] = sums[t * 8 : t * 8 + 8]

    @pl.when(step == 0)
    def _():
        @pl.when(col < HALF)
        def _():
            prepare_panel()
            prepare_columns()

        @pl.when(col >= HALF)
        def _():
            exchange()

    @pl.when(col < HALF)
    def _():
        lax.fori_loop(0, Q_STEP, one_block, 0)

        @pl.when(step == pl.num_programs(0) - 1)
        def _():
            finish()


def pair_products(blocks, panel, masks, cols, ctrial, ptrial, density, rvec, trial, window):
    shapes = [
        jax.ShapeDtypeStruct((ROWS, 8, 128), F32),
        jax.ShapeDtypeStruct((SLOTS, 8, 128), F32),
        jax.ShapeDtypeStruct((LINES, 8, 256), F32),
        jax.ShapeDtypeStruct((ROWS, 8, 128), F32),
    ]

    def whole(array):
        zeros = (0,) * len(array.shape)
        return pl.BlockSpec(array.shape, lambda i: zeros)

    operands = (panel, masks, cols, ctrial, ptrial, density, rvec, trial, window)
    return pl.pallas_call(
        pair_kernel,
        name="pairs",
        grid=(SIDE // Q_STEP,),
        out_shape=shapes,
        in_specs=[pl.BlockSpec((LINES, Q_STEP, 256, 256), lambda i: (0, i, 0, 0))]
        + [whole(x) for x in operands],
        out_specs=[whole(x) for x in shapes],
        scratch_shapes=[
            pltpu.VMEM((2, LINES * 8 * SIDE, 128), F32),
            pltpu.VMEM((2, LINES * 4 * RING, 128), F32),
            pltpu.VMEM((2, LINES * 4 * RING, 128), F32),
            pltpu.VMEM((LINES * LINES * RING, 128), F32),
            pltpu.VMEM((2, LINES * 4 * RING, 128), F32),
            pltpu.VMEM((2, SLOTS * 64, 128), F32),
            pltpu.VMEM((SLOTS * 32, 256), BF16),
            pltpu.VMEM((2, SLOTS * 32, 128), F32),
            pltpu.VMEM((2, SLOTS * 32, 128), F32),
        ],
        compiler_params=pltpu.CompilerParams(vmem_limit_bytes=48 * 1024 * 1024),
    )(blocks, *operands)


def reduce_kernel(
    zrow,
    zcol,
    pvec,
    zex,
    density,
    coulomb,
    row_image,
    col_image,
    rbuf,
    cbuf,
    dbuf,
    pbuf,
    ebuf,
    fbuf,
    ssum,
    dens_v,
    send,
    recv,
    local,
):
    row, col = lax.axis_index("row"), lax.axis_index("col")
    first = row * WIDTH
    greet()

    def to(source, target, number, arrives, device):
        return remote(source, target, send.at[number], recv.at[arrives], device)

    def row_peers():
        return [(step, lax.rem(row + step, ROWS)) for step in range(1, ROWS)]

    def row_sources():
        return [(step, lax.rem(row + ROWS - step, ROWS)) for step in range(1, ROWS)]

    def final_copies():
        copies = []
        for step in range(1, 2 * HALF):
            peer = lax.rem(col + step, 2 * HALF)
            copies.append(to(ssum, fbuf.at[col], 8 + step, 16 + col, (row, peer)))
        return copies

    @pl.when(col < HALF)
    def _():
        copies = [
            to(zrow.at[peer], rbuf.at[row], step, step, (peer, col)) for step, peer in row_peers()
        ]
        near = to(zcol.at[0:LINES], cbuf, 0, 8, (row, col + HALF))
        for copy in copies:
            copy.start()
        near.start()

        @pl.when(col < HALF - 1)
        def _():
            far = to(zcol.at[LINES:SLOTS], dbuf, 8, 9, (row, col + HALF + 1))
            far.start()
            far.wait_send()

        total = zrow[row]
        for step, source in row_sources():
            to(zrow.at[0], rbuf.at[source], 0, step, (source, col)).wait_recv()
            total += rbuf[source]
        ssum[...] = total
        for copy in copies:
            copy.wait_send()
        near.wait_send()

    @pl.when(col >= HALF)
    def _():
        copies = [
            to(zex.at[peer], ebuf.at[row], step, step, (peer, col)) for step, peer in row_peers()
        ]
        for copy in copies:
            copy.start()

        @pl.when(col > HALF)
        def _():
            part = to(pvec, pbuf.at[col - HALF], 0, 24 + col, (row, HALF))
            part.start()
            part.wait_send()

        @pl.when(col == HALF)
        def _():
            fetch = pltpu.make_async_copy(density.at[:, pl.ds(first, WIDTH)], dens_v, local.at[0])
            fetch.start()
            sums = [pvec[t] for t in range(LINES)]
            for j in range(1, HALF):
                to(pvec, pbuf.at[j], 0, 24 + HALF + j, (row, HALF)).wait_recv()
                for t in range(LINES):
                    sums[t] += pbuf[j, t]
            fetch.wait()
            total = jnp.zeros((8, 128), F32)
            lanes = WIDTH * 16
            own = iota((8, lanes), 1) // 16 == iota((8, lanes), 0)
            for t in range(LINES):
                scaled = (dens_v[t].astype(F32) * coulomb[...]).astype(BF16)
                scaled = scaled.reshape(lanes, 256)
                high = sums[t].astype(BF16)
                low = (sums[t] - high.astype(F32)).astype(BF16)
                products = dot(jnp.concatenate([high, low], axis=0), scaled, (1, 1))
                products = jnp.where(own, products[0:8] + products[8:16], 0.0)
                fold = ones_where(
                    iota((lanes, 128), 0) % 16 + t * 16 == iota((lanes, 128), 1), F32
                )
                total += dot(products, fold, precision=HIGHEST)
            ssum[...] = 2.0 * total

        for copy in copies:
            copy.wait_send()

    @pl.when(col <= HALF)
    def _():
        for copy in final_copies():
            copy.start()
        fbuf[col] = ssum[...]

    for source in range(HALF + 1):

        @pl.when(col != source)
        def _():
            to(ssum, fbuf.at[source], 0, 16 + source, (row, source)).wait_recv()

    total = fbuf[0]
    for source in range(1, HALF + 1):
        total += fbuf[source]
    choose = ones_where(iota((8, 128), 1) == iota((8, 128), 0) * 16 + col, F32)
    picked = dot(choose, total, (1, 1), HIGHEST)
    row_image[0] = picked[0:LINES, 0:WIDTH]

    @pl.when(col <= HALF)
    def _():
        for copy in final_copies():
            copy.wait_send()

    @pl.when(col < HALF)
    def _():
        col_image[...] = jnp.zeros_like(col_image)

    @pl.when(col >= HALF)
    def _():
        exchange = zex[row]
        for step, source in row_sources():
            to(zex.at[0], ebuf.at[source], 0, step, (source, col)).wait_recv()
            exchange += ebuf[source]
        to(zcol.at[0:LINES], cbuf, 0, 8, (row, HALF)).wait_recv()

        @pl.when(col > HALF)
        def _():
            to(zcol.at[LINES:SLOTS], dbuf, 0, 9, (row, HALF)).wait_recv()

        picks = ones_where(iota((16, 128), 0) == iota((16, 128), 1), F32)
        folds = iota((16, 128), 1) % 16 == iota((16, 128), 0)
        spots = ones_where(iota((8, 128), 1) // 16 == iota((8, 128), 0), F32)
        for a in range(LINES):
            direct = cbuf[a]
            if a < LINES - 1:
                direct += jnp.where(col > HALF, dbuf[a], 0.0)
            image = dot(picks, direct, (1, 1), HIGHEST)
            values = jnp.where(folds, exchange[a : a + 1], 0.0)
            image += dot(values, spots, (1, 1), HIGHEST)
            col_image[:, a, :] = image[:, 0:WIDTH]


def reduce_parts(zrow, zcol, pvec, zex, density, coulomb):
    return pl.pallas_call(
        reduce_kernel,
        name="reduce",
        out_shape=[
            jax.ShapeDtypeStruct((1, LINES, WIDTH), F32),
            jax.ShapeDtypeStruct((16, LINES, WIDTH), F32),
        ],
        in_specs=[VMEM, VMEM, VMEM, VMEM, ANY, VMEM],
        out_specs=[VMEM, VMEM],
        scratch_shapes=[
            pltpu.VMEM((ROWS, 8, 128), F32),
            pltpu.VMEM((LINES, 8, 128), F32),
            pltpu.VMEM((SLOTS - LINES, 8, 128), F32),
            pltpu.VMEM((HALF, LINES, 8, 256), F32),
            pltpu.VMEM((ROWS, 8, 128), F32),
            pltpu.VMEM((HALF + 1, 8, 128), F32),
            pltpu.VMEM((8, 128), F32),
            pltpu.VMEM((LINES, WIDTH, 16, 256), BF16),
            pltpu.SemaphoreType.DMA((24,)),
            pltpu.SemaphoreType.DMA((40,)),
            pltpu.SemaphoreType.DMA((1,)),
        ],
        compiler_params=pltpu.CompilerParams(collective_id=1, has_side_effects=True),
    )(zrow, zcol, pvec, zex, density, coulomb)


def local(band_factors, pair_density, screened, coulomb, window_mask, trial_vector):
    trial = trial_vector.transpose(1, 2, 0)
    scale = coulomb.reshape(1, 256)
    panel, masks, cols, ctrial, ptrial, rvec = gather(
        band_factors, pair_density, trial, window_mask, scale
    )
    parts = pair_products(
        screened, panel, masks, cols, ctrial, ptrial, pair_density, rvec, trial, window_mask
    )
    row_image, col_image = reduce_parts(*parts, pair_density, scale)
    return row_image, col_image


def solution(mesh):
    placed = (
        P("col", None, None, None),
        P("col", None, None, None),
        P("col", None, None, None),
        P(),
        P(None, "row", None),
        P(None, "col", None),
    )
    return jax.shard_map(
        local,
        mesh=mesh,
        in_specs=placed,
        out_specs=(P("col", None, "row"), P(None, "col", "row")),
        check_vma=False,
    )
```

```python
import functools

import jax
import jax.numpy as jnp
from jax import lax
from jax.experimental import pallas as pl
from jax.experimental.pallas import tpu as pltpu
from jax.sharding import PartitionSpec as P

MESH = pl.DeviceIdType.MESH
F32 = jnp.float32
BF16 = jnp.bfloat16
SIDE = 48
ROWS = 8
WIDTH = 6
LINES = 3
HALF = 8
SLOTS = 2 * LINES - 1
RING = SIDE + 8
Q_STEP = 4
HIGHEST = lax.Precision.HIGHEST
ANY = pl.BlockSpec(memory_space=pl.ANY)
VMEM = pl.BlockSpec(memory_space=pltpu.VMEM)


def iota(shape, axis):
    return lax.broadcasted_iota(jnp.int32, shape, axis)


def dot(a, b, contract=(1, 0), precision=None):
    return lax.dot_general(
        a,
        b,
        (((contract[0],), (contract[1],)), ((), ())),
        preferred_element_type=F32,
        precision=precision,
    )


def ones_where(condition, dtype=BF16):
    return jnp.where(condition, 1.0, 0.0).astype(dtype)


def pick_rows(trial_line, first):
    pick = ones_where(iota((8, SIDE), 1) == first + iota((8, SIDE), 0))
    return dot(pick, trial_line, (1, 1)).astype(BF16)


def block_diagonal(trial_line, first, copies):
    rows = pick_rows(trial_line, first)
    tiled = dot(rows, ones_where(iota((16, copies * 16), 1) % 16 == iota((16, copies * 16), 0)))
    return jnp.where(iota(tiled.shape, 1) // 16 == iota(tiled.shape, 0), tiled, 0.0)


def greet():
    row, col = lax.axis_index("row"), lax.axis_index("col")
    barrier = pltpu.get_barrier_semaphore()
    for step in range(1, ROWS):
        pl.semaphore_signal(
            barrier, inc=1, device_id=(lax.rem(row + step, ROWS), col), device_id_type=MESH
        )
    for step in range(1, 2 * HALF):
        pl.semaphore_signal(
            barrier, inc=1, device_id=(row, lax.rem(col + step, 2 * HALF)), device_id_type=MESH
        )
    pl.semaphore_wait(barrier, ROWS + 2 * HALF - 2)


def remote(source, target, send_sem, recv_sem, device):
    return pltpu.make_async_remote_copy(
        src_ref=source,
        dst_ref=target,
        send_sem=send_sem,
        recv_sem=recv_sem,
        device_id=device,
        device_id_type=MESH,
    )


def panel_product_kernel(
    bands,
    density,
    blocks,
    trial,
    window,
    trial_v,
    coulomb,
    row_image,
    col_image,
    w_buf,
    dens,
    pieces,
    cols,
    ctrial,
    ptrial,
    rsend,
    rvec,
    flat,
    left_t,
    y_row,
    keep_t,
    r_sum,
    col_flat,
    u_col,
    y_col,
    c_sum,
    zrow,
    zcol,
    pvec,
    zex,
    rbuf,
    cbuf,
    dbuf,
    pbuf,
    ebuf,
    fbuf,
    ssum,
    send,
    recv,
    local,
    w_sem,
):
    row, col = lax.axis_index("row"), lax.axis_index("col")
    first = row * WIDTH
    core = lax.rem(col, 2)
    twin = (row, col + 1 - 2 * core)
    halves = (slice(0, 128), slice(128, 256))
    spread = ones_where(iota((16, 2048), 1) // 128 == iota((16, 2048), 0))

    def to(source, target, number, arrives, device):
        return remote(source, target, send.at[number], recv.at[arrives], device)

    def row_peers():
        return [(step, lax.rem(row + step, ROWS)) for step in range(1, ROWS)]

    def row_sources():
        return [(step, lax.rem(row + ROWS - step, ROWS)) for step in range(1, ROWS)]

    COLS, NEXT, CT, CTN, PT, OWN, RVEC = 0, 1, 2, 3, 4, 5, 6
    PIECE, TWIN, RSUM, CSUM, DSUM, FINAL, PVEC = 8, 16, 24, 32, 33, 34, 44
    S_PIECE, S_TWIN, S_RSUM, S_CSUM, S_DSUM, S_FINAL, S_SWAP = 0, 8, 16, 24, 25, 32, 48

    def lane(expanded, s):
        return expanded[:, s * 128 : (s + 1) * 128]

    def chunk(number):
        return pltpu.make_async_copy(
            blocks.at[:, pl.ds(number * Q_STEP, Q_STEP)],
            w_buf.at[:, pl.ds(number * Q_STEP, Q_STEP)],
            w_sem.at[number],
        )

    def fetch_density():
        return pltpu.make_async_copy(density, dens, local.at[0])

    def store_ring(table, h, number, value):
        base = number * RING
        table[h, base : base + SIDE, :] = value
        table[h, base + SIDE : base + RING, :] = value[0:8]

    def unpack_piece(half, source):
        for t in range(LINES):
            value = pieces[half, source, t].astype(F32).reshape(WIDTH * 4, 256)
            base = pl.multiple_of((t * SIDE + source * WIDTH + half * (WIDTH // 2)) * 8, 8)
            for h in range(2):
                flat[h, pl.ds(base, WIDTH * 4), :] = value[:, halves[h]]

    def prepare_panel():
        for t in range(LINES):
            line = jnp.transpose(ptrial[t].astype(F32)).astype(BF16)
            expanded = dot(line, spread)
            for h in range(2):

                def band(number):
                    return flat[h, pl.ds(t * 8 * SIDE + number, SIDE, stride=8), :]

                for c in range(4):
                    store_ring(left_t, h, t * 4 + c, band(c))
                valence = [band(4 + v) for v in range(4)]
                for c in range(4):
                    total = valence[0] * lane(expanded, c)
                    for v in range(1, 4):
                        total += valence[v] * lane(expanded, 4 * v + c)
                    store_ring(y_row, h, t * 4 + c, total)
        places = iota((8, 256), 1)
        rows = iota((8, 256), 0)
        for e in range(LINES):
            line = HALF * LINES + col * LINES + e + rows
            for source in range(ROWS):
                for half in range(2):
                    for i in range(WIDTH // 2):
                        held = pieces[half, source, LINES, i].astype(F32)
                        held = jnp.where((places == line) & (rows < LINES), held, 0.0)
                        factor = jnp.sum(held, axis=1, keepdims=True)
                        factor = jnp.broadcast_to(factor, (8, 128))
                        b = source * WIDTH + half * (WIDTH // 2) + i
                        for t in range(LINES):
                            base = (e * LINES + t) * RING
                            keep_t[base + b : base + b + 1, :] = factor[t : t + 1]
                            if b < 8:
                                base += SIDE
                                keep_t[base + b : base + b + 1, :] = factor[t : t + 1]
        r_sum[...] = jnp.zeros_like(r_sum)

    def prepare_columns():
        for a in range(SLOTS):
            value = cols[a].astype(F32).reshape(WIDTH * 8, 256)
            if a >= LINES:
                value = jnp.where(col < HALF - 1, value, 0.0)
            for h in range(2):
                col_flat[h, a * 64 : a * 64 + WIDTH * 8, :] = value[:, halves[h]]
                col_flat[h, a * 64 + WIDTH * 8 : a * 64 + 64, :] = jnp.zeros((16, 128), F32)
        for a in range(SLOTS):
            line = ctrial[a // LINES, a % LINES]
            expanded = dot(pick_rows(line, first), spread)
            if a >= LINES:
                expanded = jnp.where(col < HALF - 1, expanded, 0.0)
            for h in range(2):

                def band(number):
                    return col_flat[h, pl.ds(a * 64 + number, 8, stride=8), :]

                for pair in range(2):
                    both = jnp.concatenate([band(2 * pair), band(2 * pair + 1)], axis=0)
                    u_col[a * 32 + pair * 16 : a * 32 + pair * 16 + 16, halves[h]] = both.astype(
                        BF16
                    )
                valence = [band(4 + v) for v in range(4)]
                for c in range(4):
                    total = valence[0] * lane(expanded, c)
                    for v in range(1, 4):
                        total += valence[v] * lane(expanded, 4 * v + c)
                    y_col[h, (a * 4 + c) * 8 : (a * 4 + c) * 8 + 8, :] = total
        c_sum[...] = jnp.zeros_like(c_sum)

    def one_block(q_value, carry):
        start = lax.rem(first + SIDE - q_value, SIDE)
        inside = (first + iota((8, 128), 0) >= q_value) | (col > 0)
        same = (q_value == 0) & (col == 0)
        for t in range(LINES):

            def rows(table, c, h):
                return table[h, pl.ds((t * 4 + c) * RING + start, 8), :]

            lefts = [[rows(left_t, c, h) for h in range(2)] for c in range(4)]
            backs = [[rows(y_row, c, h) for h in range(2)] for c in range(4)]
            totals = [[None, None] for _ in range(4)]
            for e in range(LINES):
                a = t + e
                factor = keep_t[pl.ds((e * LINES + t) * RING + start, 8), :]
                if e == 0:
                    factor = jnp.where(inside, factor, 0.0)
                tiles = []
                for c in range(4):
                    both = []
                    for h in range(2):
                        kept = lefts[c][h] * factor
                        both.append(jnp.concatenate([kept, kept], axis=0).astype(BF16))
                    both = jnp.concatenate(both, axis=1)
                    for pair in range(2):
                        base = a * 32 + pair * 16
                        tiles.append(both * u_col[base : base + 16, :])
                mixed = dot(jnp.concatenate(tiles, axis=0), w_buf[e, q_value])
                for h in range(2):
                    images = [None] * 4
                    for c in range(4):
                        for d in range(4):
                            base = (c * 4 + d) * 8
                            piece = mixed[base : base + 8, halves[h]]
                            base = (a * 4 + d) * 8
                            part = piece * y_col[h, base : base + 8, :]
                            totals[c][h] = part if totals[c][h] is None else totals[c][h] + part
                            part = piece * backs[c][h]
                            images[d] = part if images[d] is None else images[d] + part
                    for d in range(4):
                        base = (a * 4 + d) * 8
                        image = jnp.where(same, 0.0, images[d]) if e == 0 else images[d]
                        c_sum[h, base : base + 8, :] += image
            for c in range(4):
                for h in range(2):
                    r_sum[h, pl.ds((t * 4 + c) * RING + start, 8), :] += totals[c][h]
        return carry

    def finish():
        lanes = iota((SIDE, 128), 1)
        image = jnp.zeros((SIDE, 128), F32)
        for t in range(LINES):
            for c in range(4):
                base = (t * 4 + c) * RING
                total = []
                for h in range(2):
                    head = r_sum[h, base : base + 8, :] + r_sum[h, base + SIDE : base + RING, :]
                    total.append(
                        jnp.concatenate([head, r_sum[h, base + 8 : base + SIDE, :]], axis=0)
                    )
                for v in range(4):
                    product = 0.0
                    for h in range(2):
                        strided = pl.ds(t * 8 * SIDE + 4 + v, SIDE, stride=8)
                        product += flat[h, strided, :] * total[h]
                    value = jnp.sum(product, axis=1, keepdims=True)
                    image = jnp.where(lanes == t * 16 + 4 * v + c, value, image)
        for target in range(ROWS):
            zrow[target, 0:WIDTH, :] = -image[target * WIDTH : (target + 1) * WIDTH]
            zrow[target, WIDTH:8, :] = jnp.zeros((8 - WIDTH, 128), F32)
        lanes = iota((8, 128), 1)
        for a in range(SLOTS):
            image = jnp.zeros((8, 128), F32)
            for v in range(4):
                for c in range(4):
                    product = 0.0
                    for h in range(2):
                        base = (a * 4 + c) * 8
                        strided = pl.ds(a * 64 + 4 + v, 8, stride=8)
                        product += col_flat[h, strided, :] * c_sum[h, base : base + 8, :]
                    value = jnp.sum(product, axis=1, keepdims=True)
                    image = jnp.where(lanes == 4 * v + c, value, image)
            zcol[a] = -image

    def exchange():
        tile = ones_where(iota((16, SIDE * 16), 1) % 16 == iota((16, SIDE * 16), 0))
        own_point = iota((SIDE, SIDE * 16), 1) // 16 == iota((SIDE, SIDE * 16), 0)
        ones = jnp.ones((8, SIDE), BF16)
        points = iota((8, SIDE * 16), 1) // 16
        row_points = first + iota((8, SIDE * 16), 0)
        places = iota((WIDTH, SIDE), 1)
        wide = jnp.concatenate([rvec[t] for t in range(LINES)], axis=0)
        high = wide.astype(BF16)
        low = (wide - high.astype(F32)).astype(BF16)
        split = jnp.concatenate([high, low], axis=0)
        zex[...] = jnp.zeros_like(zex)
        sums = jnp.zeros((8 * LINES, 256), F32)
        for a in range(LINES):
            line = col * LINES + a
            transposed = jnp.transpose(trial_v[a].astype(F32)).astype(BF16)
            values = jnp.where(own_point, dot(transposed, tile), 0.0).astype(BF16)
            values = dot(ones, values)
            kept_values = []
            strict_factors = []
            for t in range(LINES):
                row_line = HALF * LINES + t
                held = jnp.where(places == line, window[t], 0).astype(F32)
                held = jnp.sum(held, axis=1, keepdims=True)
                held = jnp.concatenate([held, jnp.zeros((8 - WIDTH, 1), F32)], axis=0)
                kept = (line > row_line) | ((line == row_line) & (points >= row_points))
                strict = (line > row_line) | ((line == row_line) & (points > row_points))
                kept_values.append(jnp.where(kept, held, 0.0) * values)
                strict_factors.append(jnp.where(strict, held, 0.0))
            table = dens[a].reshape(SIDE * 16, 256)
            sums += dot(jnp.concatenate(kept_values, axis=0).astype(BF16), table)
            products = dot(split, table, (1, 1))
            products = products[0 : 8 * LINES] + products[8 * LINES : 16 * LINES]
            image = jnp.sum(
                products * jnp.concatenate(strict_factors, axis=0), axis=0, keepdims=True
            )
            for target in range(ROWS):
                lanes = slice(target * WIDTH * 16, (target + 1) * WIDTH * 16)
                zex[target, a : a + 1, 0 : WIDTH * 16] = 2.0 * image[:, lanes]
        for t in range(LINES):
            pvec[t] = sums[t * 8 : t * 8 + 8]

    def row_vectors():
        for t in range(LINES):
            diagonal = block_diagonal(trial_v[t], first, WIDTH).astype(BF16)
            scaled = (dens[t, pl.ds(first, WIDTH)].astype(F32) * coulomb[...]).astype(BF16)
            rsend[t] = dot(diagonal, scaled.reshape(WIDTH * 16, 256))

    def exchange_rows():
        total = jnp.zeros((8, 128), F32)
        lanes = WIDTH * 16
        own = iota((8, lanes), 1) // 16 == iota((8, lanes), 0)
        for t in range(LINES):
            summed = pvec[t]
            for j in range(1, HALF):
                summed += pbuf[j, t]
            scaled = (dens[t, pl.ds(first, WIDTH)].astype(F32) * coulomb[...]).astype(BF16)
            scaled = scaled.reshape(lanes, 256)
            high = summed.astype(BF16)
            low = (summed - high.astype(F32)).astype(BF16)
            products = dot(jnp.concatenate([high, low], axis=0), scaled, (1, 1))
            products = jnp.where(own, products[0:8] + products[8:16], 0.0)
            fold = ones_where(iota((lanes, 128), 0) % 16 + t * 16 == iota((lanes, 128), 1), F32)
            total += dot(products, fold, precision=HIGHEST)
        ssum[...] = 2.0 * total

    def final_copies():
        copies = []
        for step in range(1, 2 * HALF):
            peer = lax.rem(col + step, 2 * HALF)
            copies.append(to(ssum, fbuf.at[col], S_FINAL + step, FINAL + col, (row, peer)))
        return copies

    def half_panel(half):
        return bands.at[:, pl.ds(first + half * (WIDTH // 2), WIDTH // 2)]

    def panel_copies():
        return [
            to(half_panel(j % 2), pieces.at[j % 2, row, 0:LINES], j, OWN, (row, j))
            for j in range(HALF)
        ] + [to(trial, ptrial, 8 + j, PT, (row, j)) for j in range(HALF)]

    def column_copies():
        near = (row, lax.rem(col + HALF, 2 * HALF))
        own = bands.at[:, pl.ds(first, WIDTH)]
        return [
            to(own, cols.at[0:LINES], 16, COLS, near),
            to(trial, ctrial.at[0], 17, CT, near),
        ]

    def next_copies():
        far = (row, lax.rem(col + HALF - 1, 2 * HALF))
        own = bands.at[0 : LINES - 1, pl.ds(first, WIDTH)]
        return [
            to(own, cols.at[LINES:SLOTS], 18, NEXT, far),
            to(trial, ctrial.at[1], 19, CTN, far),
        ]

    def vector_copies():
        return [to(rsend, rvec, 20 + j, RVEC, (row, HALF + j)) for j in range(1, HALF)]

    def piece_copies():
        own = pieces.at[core, row]
        return [to(own, own, S_TWIN, TWIN, twin)] + [
            to(own, own, S_PIECE + step, PIECE + step, (peer, col)) for step, peer in row_peers()
        ]

    def twin_copies():
        return [
            to(pieces.at[core, source], pieces.at[core, source], S_TWIN + step, TWIN + step, twin)
            for step, source in row_sources()
        ]

    def sum_copies():
        return [
            to(zrow.at[peer], rbuf.at[row], S_RSUM + step, RSUM + step, (peer, col))
            for step, peer in row_peers()
        ]

    def near_sum():
        return to(zcol.at[0:LINES], cbuf, S_CSUM, CSUM, (row, lax.rem(col + HALF, 2 * HALF)))

    def far_sum():
        return to(
            zcol.at[LINES:SLOTS], dbuf, S_DSUM, DSUM, (row, lax.rem(col + HALF + 1, 2 * HALF))
        )

    def exchange_copies():
        return [
            to(zex.at[peer], ebuf.at[row], S_SWAP + step, RSUM + step, (peer, col))
            for step, peer in row_peers()
        ]

    def part_copy():
        return to(pvec, pbuf.at[col - HALF], 8, PVEC + col - HALF, (row, HALF))

    @pl.when(col < HALF)
    def _():
        for number in range(SIDE // Q_STEP):
            chunk(number).start()
        for i in range(WIDTH // 2):
            held = jnp.where(core == 0, window[:, i], window[:, WIDTH // 2 + i]).astype(F32)
            held = jnp.concatenate([held, jnp.zeros((8 - LINES, SIDE), F32)], axis=0)
            held = jnp.concatenate([held, jnp.zeros((8, 256 - SIDE), F32)], axis=1)
            pieces[core, row, LINES, i] = held.astype(BF16)

    @pl.when(col >= HALF)
    def _():
        fetch_density().start()

    greet()

    @pl.when(col < HALF)
    def _():
        to(half_panel(0), pieces.at[core, row, 0:LINES], 0, OWN, (row, HALF)).wait_recv()
        for copy in piece_copies():
            copy.start()
        to(cols.at[0:LINES], cols.at[0:LINES], 0, COLS, (row, HALF)).wait_recv()
        to(trial, ctrial.at[0], 0, CT, (row, HALF)).wait_recv()

        @pl.when(col < HALF - 1)
        def _():
            to(cols.at[LINES:SLOTS], cols.at[LINES:SLOTS], 0, NEXT, (row, HALF)).wait_recv()
            to(trial, ctrial.at[1], 0, CTN, (row, HALF)).wait_recv()

        prepare_columns()
        unpack_piece(core, row)
        forwards = twin_copies()
        for (step, source), forward in zip(row_sources(), forwards):
            piece = pieces.at[core, source]
            to(piece, piece, 0, PIECE + step, (source, col)).wait_recv()
            forward.start()
            unpack_piece(core, source)
        piece = pieces.at[1 - core, row]
        to(piece, piece, 0, TWIN, twin).wait_recv()
        unpack_piece(1 - core, row)
        for step, source in row_sources():
            piece = pieces.at[1 - core, source]
            to(piece, piece, 0, TWIN + step, twin).wait_recv()
            unpack_piece(1 - core, source)
        to(trial, ptrial, 0, PT, (row, HALF)).wait_recv()
        prepare_panel()

        def one_chunk(number, carry):
            chunk(number).wait()
            return lax.fori_loop(number * Q_STEP, (number + 1) * Q_STEP, one_block, carry)

        lax.fori_loop(0, SIDE // Q_STEP, one_chunk, 0)
        finish()
        for copy in sum_copies():
            copy.start()
        near_sum().start()

        @pl.when(col < HALF - 1)
        def _():
            far_sum().start()

        total = zrow[row]
        for step, source in row_sources():
            to(zrow.at[0], rbuf.at[source], 0, RSUM + step, (source, col)).wait_recv()
            total += rbuf[source]
        ssum[...] = total

    @pl.when(col >= HALF)
    def _():
        @pl.when(col == HALF)
        def _():
            for copy in panel_copies():
                copy.start()

        for copy in column_copies():
            copy.start()

        @pl.when(col > HALF)
        def _():
            for copy in next_copies():
                copy.start()

        fetch_density().wait()

        @pl.when(col == HALF)
        def _():
            row_vectors()
            for copy in vector_copies():
                copy.start()
            rvec[...] = rsend[...]

        @pl.when(col > HALF)
        def _():
            to(rsend, rvec, 0, RVEC, (row, HALF)).wait_recv()

        exchange()
        for copy in exchange_copies():
            copy.start()

        @pl.when(col > HALF)
        def _():
            part_copy().start()

        @pl.when(col == HALF)
        def _():
            for j in range(1, HALF):
                to(pvec, pbuf.at[j], 0, PVEC + j, (row, HALF)).wait_recv()
            exchange_rows()

    @pl.when(col <= HALF)
    def _():
        for copy in final_copies():
            copy.start()
        fbuf[col] = ssum[...]

    @pl.when(col < HALF)
    def _():
        col_image[...] = jnp.zeros_like(col_image)

    @pl.when(col >= HALF)
    def _():
        swapped = zex[row]
        for step, source in row_sources():
            to(zex.at[0], ebuf.at[source], 0, RSUM + step, (source, col)).wait_recv()
            swapped += ebuf[source]
        to(zcol.at[0:LINES], cbuf, 0, CSUM, (row, HALF)).wait_recv()

        @pl.when(col > HALF)
        def _():
            to(zcol.at[LINES:SLOTS], dbuf, 0, DSUM, (row, HALF)).wait_recv()

        picks = ones_where(iota((16, 128), 0) == iota((16, 128), 1), F32)
        folds = iota((16, 128), 1) % 16 == iota((16, 128), 0)
        spots = ones_where(iota((8, 128), 1) // 16 == iota((8, 128), 0), F32)
        for a in range(LINES):
            direct = cbuf[a]
            if a < LINES - 1:
                direct += jnp.where(col > HALF, dbuf[a], 0.0)
            image = dot(picks, direct, (1, 1), HIGHEST)
            values = jnp.where(folds, swapped[a : a + 1], 0.0)
            image += dot(values, spots, (1, 1), HIGHEST)
            col_image[:, a, :] = image[:, 0:WIDTH]

    for source in range(HALF + 1):

        @pl.when(col != source)
        def _():
            to(ssum, fbuf.at[source], 0, FINAL + source, (row, source)).wait_recv()

    total = fbuf[0]
    for source in range(1, HALF + 1):
        total += fbuf[source]
    choose = ones_where(iota((8, 128), 1) == iota((8, 128), 0) * 16 + col, F32)
    picked = dot(choose, total, (1, 1), HIGHEST)
    row_image[0] = picked[0:LINES, 0:WIDTH]

    @pl.when(col < HALF)
    def _():
        for copy in piece_copies() + twin_copies() + sum_copies() + [near_sum()]:
            copy.wait_send()

        @pl.when(col < HALF - 1)
        def _():
            far_sum().wait_send()

    @pl.when(col >= HALF)
    def _():
        for copy in column_copies() + exchange_copies():
            copy.wait_send()

        @pl.when(col > HALF)
        def _():
            for copy in next_copies() + [part_copy()]:
                copy.wait_send()

        @pl.when(col == HALF)
        def _():
            for copy in panel_copies() + vector_copies():
                copy.wait_send()

    @pl.when(col <= HALF)
    def _():
        for copy in final_copies():
            copy.wait_send()


def local(band_factors, pair_density, screened, coulomb, window_mask, trial_vector):
    trial = trial_vector.transpose(1, 0, 2)
    vmem = pltpu.VMEM
    row_image, col_image = pl.pallas_call(
        panel_product_kernel,
        name="panel_product",
        out_shape=[
            jax.ShapeDtypeStruct((1, LINES, WIDTH), F32),
            jax.ShapeDtypeStruct((16, LINES, WIDTH), F32),
        ],
        in_specs=[ANY, ANY, ANY, ANY, VMEM, VMEM, VMEM],
        out_specs=[VMEM, VMEM],
        scratch_shapes=[
            vmem((LINES, SIDE, 256, 256), BF16),
            vmem((LINES, SIDE, 16, 256), BF16),
            vmem((2, ROWS, LINES + 1, WIDTH // 2, 8, 256), BF16),
            vmem((SLOTS, WIDTH, 8, 256), BF16),
            vmem((2, LINES, 16, SIDE), BF16),
            vmem((LINES, 16, SIDE), BF16),
            vmem((LINES, 8, 256), F32),
            vmem((LINES, 8, 256), F32),
            vmem((2, LINES * 8 * SIDE, 128), F32),
            vmem((2, LINES * 4 * RING, 128), F32),
            vmem((2, LINES * 4 * RING, 128), F32),
            vmem((LINES * LINES * RING, 128), F32),
            vmem((2, LINES * 4 * RING, 128), F32),
            vmem((2, SLOTS * 64, 128), F32),
            vmem((SLOTS * 32, 256), BF16),
            vmem((2, SLOTS * 32, 128), F32),
            vmem((2, SLOTS * 32, 128), F32),
            vmem((ROWS, 8, 128), F32),
            vmem((SLOTS, 8, 128), F32),
            vmem((LINES, 8, 256), F32),
            vmem((ROWS, 8, 128), F32),
            vmem((ROWS, 8, 128), F32),
            vmem((LINES, 8, 128), F32),
            vmem((SLOTS - LINES, 8, 128), F32),
            vmem((HALF, LINES, 8, 256), F32),
            vmem((ROWS, 8, 128), F32),
            vmem((HALF + 1, 8, 128), F32),
            vmem((8, 128), F32),
            pltpu.SemaphoreType.DMA((56,)),
            pltpu.SemaphoreType.DMA((52,)),
            pltpu.SemaphoreType.DMA((1,)),
            pltpu.SemaphoreType.DMA((SIDE // Q_STEP,)),
        ],
        compiler_params=pltpu.CompilerParams(
            collective_id=0, has_side_effects=True, vmem_limit_bytes=56 * 1024 * 1024
        ),
    )(
        band_factors,
        pair_density,
        screened,
        trial,
        window_mask,
        trial,
        coulomb.reshape(1, 256),
    )
    return row_image, col_image


def solution(mesh):
    placed = (
        P("col", None, None, None),
        P("col", None, None, None),
        P("col", None, None, None),
        P(),
        P(None, "row", None),
        P(None, "col", None),
    )
    return jax.shard_map(
        local,
        mesh=mesh,
        in_specs=placed,
        out_specs=(P("col", None, "row"), P(None, "col", "row")),
        check_vma=False,
    )
```

```python
import functools

import jax
import jax.numpy as jnp
from jax import lax
from jax.experimental import pallas as pl
from jax.experimental.pallas import tpu as pltpu
from jax.sharding import PartitionSpec as P

MESH = pl.DeviceIdType.MESH
F32 = jnp.float32
BF16 = jnp.bfloat16
SIDE = 48
ROWS = 8
WIDTH = 6
LINES = 3
HALF = 8
SLOTS = 2 * LINES - 1
RING = SIDE + 8
BLOCKS = LINES * WIDTH // 2 + 1
Q_STEP = 4
HIGHEST = lax.Precision.HIGHEST
ANY = pl.BlockSpec(memory_space=pl.ANY)
VMEM = pl.BlockSpec(memory_space=pltpu.VMEM)


def iota(shape, axis):
    return lax.broadcasted_iota(jnp.int32, shape, axis)


def dot(a, b, contract=(1, 0), precision=None):
    return lax.dot_general(
        a,
        b,
        (((contract[0],), (contract[1],)), ((), ())),
        preferred_element_type=F32,
        precision=precision,
    )


def ones_where(condition, dtype=BF16):
    return jnp.where(condition, 1.0, 0.0).astype(dtype)


def pick_rows(trial_line, first):
    pick = ones_where(iota((8, SIDE), 1) == first + iota((8, SIDE), 0))
    return dot(pick, trial_line, (1, 1)).astype(BF16)


def block_diagonal(trial_line, first, copies):
    rows = pick_rows(trial_line, first)
    tiled = dot(rows, ones_where(iota((16, copies * 16), 1) % 16 == iota((16, copies * 16), 0)))
    return jnp.where(iota(tiled.shape, 1) // 16 == iota(tiled.shape, 0), tiled, 0.0)


def greet():
    row, col = lax.axis_index("row"), lax.axis_index("col")
    barrier = pltpu.get_barrier_semaphore()
    for step in range(1, ROWS):
        pl.semaphore_signal(
            barrier, inc=1, device_id=(lax.rem(row + step, ROWS), col), device_id_type=MESH
        )
    for step in range(1, 2 * HALF):
        pl.semaphore_signal(
            barrier, inc=1, device_id=(row, lax.rem(col + step, 2 * HALF)), device_id_type=MESH
        )
    pl.semaphore_wait(barrier, ROWS + 2 * HALF - 2)


def remote(source, target, send_sem, recv_sem, device):
    return pltpu.make_async_remote_copy(
        src_ref=source,
        dst_ref=target,
        send_sem=send_sem,
        recv_sem=recv_sem,
        device_id=device,
        device_id_type=MESH,
    )


def panel_product_kernel(
    bands,
    density,
    blocks,
    trial,
    window,
    trial_v,
    coulomb,
    row_part,
    col_part,
    w_buf,
    dens,
    stage,
    pieces,
    cols,
    ctrial,
    ptrial,
    rsend,
    rvec,
    flat,
    left_t,
    y_row,
    keep_t,
    r_sum,
    col_flat,
    u_col,
    y_col,
    c_sum,
    zrow,
    zcol,
    pvec,
    zex,
    rbuf,
    cbuf,
    dbuf,
    pbuf,
    ebuf,
    fbuf,
    ssum,
    send,
    recv,
    local,
    w_sem,
):
    row, col = lax.axis_index("row"), lax.axis_index("col")
    first = row * WIDTH
    core = lax.rem(col, 2)
    twin = (row, col + 1 - 2 * core)
    halves = (slice(0, 128), slice(128, 256))
    spread = ones_where(iota((16, 2048), 1) // 128 == iota((16, 2048), 0))

    def to(source, target, number, arrives, device):
        return remote(source, target, send.at[number], recv.at[arrives], device)

    def row_peers():
        return [(step, lax.rem(row + step, ROWS)) for step in range(1, ROWS)]

    def row_sources():
        return [(step, lax.rem(row + ROWS - step, ROWS)) for step in range(1, ROWS)]

    COLS, NEXT, CT, CTN, PT, OWN, RVEC, TWIN, PIECE = 0, 1, 2, 3, 4, 5, 6, 7, 8
    RSUM, CSUM, DSUM, FINAL, PVEC = 16, 17, 18, 19, 20
    S_PIECE, S_TWIN, S_RSUM, S_CSUM, S_DSUM, S_FINAL, S_SWAP = 0, 1, 2, 3, 4, 5, 6
    S_PANEL, S_TRIAL, S_VECTOR, S_PART, S_COLUMN = 7, 8, 16, 24, 25

    def lane(expanded, s):
        return expanded[:, s * 128 : (s + 1) * 128]

    def chunk(number):
        return pltpu.make_async_copy(
            blocks.at[:, pl.ds(number * Q_STEP, Q_STEP)],
            w_buf.at[:, pl.ds(number * Q_STEP, Q_STEP)],
            w_sem.at[number],
        )

    def stage_copies():
        copies = []
        for half in range(2):
            for t in range(LINES):
                source = bands.at[t, pl.ds(first + half * (WIDTH // 2), WIDTH // 2)]
                number = half * LINES + t
                place = stage.at[half, pl.ds(t * (WIDTH // 2), WIDTH // 2)]
                copies.append(pltpu.make_async_copy(source, place, local.at[1 + number]))
        return copies

    def fetch_density():
        return pltpu.make_async_copy(density, dens, local.at[0])

    def store_ring(table, h, number, value):
        base = number * RING
        table[h, base : base + SIDE, :] = value
        table[h, base + SIDE : base + RING, :] = value[0:8]

    def unpack_piece(half, source):
        for t in range(LINES):
            lines = slice(t * (WIDTH // 2), (t + 1) * (WIDTH // 2))
            value = pieces[half, source, lines].astype(F32).reshape(WIDTH * 4, 256)
            base = pl.multiple_of((t * SIDE + source * WIDTH + half * (WIDTH // 2)) * 8, 8)
            for h in range(2):
                flat[h, pl.ds(base, WIDTH * 4), :] = value[:, halves[h]]

    def prepare_panel():
        for t in range(LINES):
            line = jnp.transpose(ptrial[t].astype(F32)).astype(BF16)
            expanded = dot(line, spread)
            for h in range(2):

                def band(number):
                    return flat[h, pl.ds(t * 8 * SIDE + number, SIDE, stride=8), :]

                for c in range(4):
                    store_ring(left_t, h, t * 4 + c, band(c))
                valence = [band(4 + v) for v in range(4)]
                for c in range(4):
                    total = valence[0] * lane(expanded, c)
                    for v in range(1, 4):
                        total += valence[v] * lane(expanded, 4 * v + c)
                    store_ring(y_row, h, t * 4 + c, total)
        places = iota((8, 256), 1)
        rows = iota((8, 256), 0)
        for e in range(LINES):
            line = HALF * LINES + col * LINES + e + rows
            for source in range(ROWS):
                for half in range(2):
                    wide = pieces[half, source, BLOCKS - 1].astype(F32)
                    for i in range(WIDTH // 2):
                        held = jnp.where((places == line + 64 * i) & (rows < LINES), wide, 0.0)
                        factor = jnp.sum(held, axis=1, keepdims=True)
                        factor = jnp.broadcast_to(factor, (8, 128))
                        b = source * WIDTH + half * (WIDTH // 2) + i
                        for t in range(LINES):
                            base = (e * LINES + t) * RING
                            keep_t[base + b : base + b + 1, :] = factor[t : t + 1]
                            if b < 8:
                                base += SIDE
                                keep_t[base + b : base + b + 1, :] = factor[t : t + 1]
        r_sum[...] = jnp.zeros_like(r_sum)

    def prepare_columns():
        for a in range(SLOTS):
            value = cols[a].astype(F32).reshape(WIDTH * 8, 256)
            if a >= LINES:
                value = jnp.where(col < HALF - 1, value, 0.0)
            for h in range(2):
                col_flat[h, a * 64 : a * 64 + WIDTH * 8, :] = value[:, halves[h]]
                col_flat[h, a * 64 + WIDTH * 8 : a * 64 + 64, :] = jnp.zeros((16, 128), F32)
        for a in range(SLOTS):
            line = ctrial[a // LINES, a % LINES]
            expanded = dot(pick_rows(line, first), spread)
            if a >= LINES:
                expanded = jnp.where(col < HALF - 1, expanded, 0.0)
            for h in range(2):

                def band(number):
                    return col_flat[h, pl.ds(a * 64 + number, 8, stride=8), :]

                for pair in range(2):
                    both = jnp.concatenate([band(2 * pair), band(2 * pair + 1)], axis=0)
                    u_col[a * 32 + pair * 16 : a * 32 + pair * 16 + 16, halves[h]] = both.astype(
                        BF16
                    )
                valence = [band(4 + v) for v in range(4)]
                for c in range(4):
                    total = valence[0] * lane(expanded, c)
                    for v in range(1, 4):
                        total += valence[v] * lane(expanded, 4 * v + c)
                    y_col[h, (a * 4 + c) * 8 : (a * 4 + c) * 8 + 8, :] = total
        c_sum[...] = jnp.zeros_like(c_sum)

    def one_block(q_value):
        start = lax.rem(first + SIDE - q_value, SIDE)
        inside = (first + iota((8, 128), 0) >= q_value) | (col > 0)
        same = (q_value == 0) & (col == 0)

        def rows(table, t, c, h):
            return table[h, pl.ds((t * 4 + c) * RING + start, 8), :]

        for e in range(LINES):
            tiles = []
            for t in range(LINES):
                a = t + e
                factor = keep_t[pl.ds((e * LINES + t) * RING + start, 8), :]
                if e == 0:
                    factor = jnp.where(inside, factor, 0.0)
                for c in range(4):
                    both = []
                    for h in range(2):
                        kept = rows(left_t, t, c, h) * factor
                        both.append(jnp.concatenate([kept, kept], axis=0).astype(BF16))
                    both = jnp.concatenate(both, axis=1)
                    for pair in range(2):
                        base = a * 32 + pair * 16
                        tiles.append(both * u_col[base : base + 16, :])
            mixed = dot(jnp.concatenate(tiles, axis=0), w_buf[e, q_value])
            for t in range(LINES):
                a = t + e
                for h in range(2):
                    images = [None] * 4
                    for c in range(4):
                        total = None
                        back = rows(y_row, t, c, h)
                        for d in range(4):
                            base = t * 128 + (c * 4 + d) * 8
                            piece = mixed[base : base + 8, halves[h]]
                            base = (a * 4 + d) * 8
                            part = piece * y_col[h, base : base + 8, :]
                            total = part if total is None else total + part
                            part = piece * back
                            images[d] = part if images[d] is None else images[d] + part
                        r_sum[h, pl.ds((t * 4 + c) * RING + start, 8), :] += total
                    for d in range(4):
                        base = (a * 4 + d) * 8
                        image = jnp.where(same, 0.0, images[d]) if e == 0 else images[d]
                        c_sum[h, base : base + 8, :] += image

    def finish():
        lanes = iota((SIDE, 128), 1)
        image = jnp.zeros((SIDE, 128), F32)
        for t in range(LINES):
            for c in range(4):
                base = (t * 4 + c) * RING
                total = []
                for h in range(2):
                    head = r_sum[h, base : base + 8, :] + r_sum[h, base + SIDE : base + RING, :]
                    total.append(
                        jnp.concatenate([head, r_sum[h, base + 8 : base + SIDE, :]], axis=0)
                    )
                for v in range(4):
                    product = 0.0
                    for h in range(2):
                        strided = pl.ds(t * 8 * SIDE + 4 + v, SIDE, stride=8)
                        product += flat[h, strided, :] * total[h]
                    value = jnp.sum(product, axis=1, keepdims=True)
                    image = jnp.where(lanes == t * 16 + 4 * v + c, value, image)
        for target in range(ROWS):
            zrow[target, 0:WIDTH, :] = -image[target * WIDTH : (target + 1) * WIDTH]
            zrow[target, WIDTH:8, :] = jnp.zeros((8 - WIDTH, 128), F32)
        lanes = iota((8, 128), 1)
        for a in range(SLOTS):
            image = jnp.zeros((8, 128), F32)
            for v in range(4):
                for c in range(4):
                    product = 0.0
                    for h in range(2):
                        base = (a * 4 + c) * 8
                        strided = pl.ds(a * 64 + 4 + v, 8, stride=8)
                        product += col_flat[h, strided, :] * c_sum[h, base : base + 8, :]
                    value = jnp.sum(product, axis=1, keepdims=True)
                    image = jnp.where(lanes == 4 * v + c, value, image)
            zcol[a] = -image

    def exchange():
        tile = ones_where(iota((16, SIDE * 16), 1) % 16 == iota((16, SIDE * 16), 0))
        own_point = iota((SIDE, SIDE * 16), 1) // 16 == iota((SIDE, SIDE * 16), 0)
        ones = jnp.ones((8, SIDE), BF16)
        points = iota((8, SIDE * 16), 1) // 16
        row_points = first + iota((8, SIDE * 16), 0)
        places = iota((WIDTH, SIDE), 1)
        wide = jnp.concatenate([rvec[t] for t in range(LINES)], axis=0)
        high = wide.astype(BF16)
        low = (wide - high.astype(F32)).astype(BF16)
        split = jnp.concatenate([high, low], axis=0)
        zex[...] = jnp.zeros_like(zex)
        sums = jnp.zeros((8 * LINES, 256), F32)
        for a in range(LINES):
            line = col * LINES + a
            transposed = jnp.transpose(trial_v[a].astype(F32)).astype(BF16)
            values = jnp.where(own_point, dot(transposed, tile), 0.0).astype(BF16)
            values = dot(ones, values)
            kept_values = []
            strict_factors = []
            for t in range(LINES):
                row_line = HALF * LINES + t
                held = jnp.where(places == line, window[t], 0).astype(F32)
                held = jnp.sum(held, axis=1, keepdims=True)
                held = jnp.concatenate([held, jnp.zeros((8 - WIDTH, 1), F32)], axis=0)
                kept = (line > row_line) | ((line == row_line) & (points >= row_points))
                strict = (line > row_line) | ((line == row_line) & (points > row_points))
                kept_values.append(jnp.where(kept, held, 0.0) * values)
                strict_factors.append(jnp.where(strict, held, 0.0))
            table = dens[a].reshape(SIDE * 16, 256)
            sums += dot(jnp.concatenate(kept_values, axis=0).astype(BF16), table)
            products = dot(split, table, (1, 1))
            products = products[0 : 8 * LINES] + products[8 * LINES : 16 * LINES]
            image = jnp.sum(
                products * jnp.concatenate(strict_factors, axis=0), axis=0, keepdims=True
            )
            for target in range(ROWS):
                lanes = slice(target * WIDTH * 16, (target + 1) * WIDTH * 16)
                zex[target, a : a + 1, 0 : WIDTH * 16] = 2.0 * image[:, lanes]
        for t in range(LINES):
            pvec[t] = sums[t * 8 : t * 8 + 8]

    def row_vectors():
        for t in range(LINES):
            diagonal = block_diagonal(trial_v[t], first, WIDTH).astype(BF16)
            scaled = (dens[t, pl.ds(first, WIDTH)].astype(F32) * coulomb[...]).astype(BF16)
            rsend[t] = dot(diagonal, scaled.reshape(WIDTH * 16, 256))

    def exchange_rows():
        total = jnp.zeros((8, 128), F32)
        lanes = WIDTH * 16
        own = iota((8, lanes), 1) // 16 == iota((8, lanes), 0)
        for t in range(LINES):
            summed = pvec[t]
            for j in range(1, HALF):
                summed += pbuf[j, t]
            scaled = (dens[t, pl.ds(first, WIDTH)].astype(F32) * coulomb[...]).astype(BF16)
            scaled = scaled.reshape(lanes, 256)
            high = summed.astype(BF16)
            low = (summed - high.astype(F32)).astype(BF16)
            products = dot(jnp.concatenate([high, low], axis=0), scaled, (1, 1))
            products = jnp.where(own, products[0:8] + products[8:16], 0.0)
            fold = ones_where(iota((lanes, 128), 0) % 16 + t * 16 == iota((lanes, 128), 1), F32)
            total += dot(products, fold, precision=HIGHEST)
        ssum[...] = 2.0 * total

    def final_copies():
        copies = []
        for step in range(1, 2 * HALF):
            peer = lax.rem(col + step, 2 * HALF)
            copies.append(to(ssum, fbuf.at[col], S_FINAL, FINAL, (row, peer)))
        return copies

    def panel_copies():
        return [to(stage.at[j % 2], pieces.at[j % 2, row], S_PANEL, OWN, (row, j)) for j in range(HALF)]

    def trial_copies():
        return [to(trial, ptrial, S_TRIAL + j, PT, (row, j)) for j in range(HALF)]

    def column_copies():
        near = (row, lax.rem(col + HALF, 2 * HALF))
        own = bands.at[:, pl.ds(first, WIDTH)]
        return [
            to(own, cols.at[0:LINES], S_COLUMN, COLS, near),
            to(trial, ctrial.at[0], S_COLUMN + 1, CT, near),
        ]

    def next_copies():
        far = (row, lax.rem(col + HALF - 1, 2 * HALF))
        own = bands.at[0 : LINES - 1, pl.ds(first, WIDTH)]
        return [
            to(own, cols.at[LINES:SLOTS], S_COLUMN + 2, NEXT, far),
            to(trial, ctrial.at[1], S_COLUMN + 3, CTN, far),
        ]

    def vector_copies():
        return [to(rsend, rvec, S_VECTOR + j, RVEC, (row, HALF + j)) for j in range(1, HALF)]

    def piece_copies():
        own = pieces.at[core, row]
        return [
            to(own, own, S_PIECE, PIECE + step, (peer, col)) for step, peer in row_peers()
        ] + [to(own, own, S_TWIN, TWIN, twin)]

    def twin_copies():
        return [
            to(pieces.at[core, source], pieces.at[core, source], S_TWIN, TWIN, twin)
            for step, source in row_sources()
        ]

    def sum_copies():
        return [
            to(zrow.at[peer], rbuf.at[step - 1], S_RSUM, RSUM, (peer, col))
            for step, peer in row_peers()
        ]

    def near_sum():
        return to(zcol.at[0:LINES], cbuf, S_CSUM, CSUM, (row, lax.rem(col + HALF, 2 * HALF)))

    def far_sum():
        return to(
            zcol.at[LINES:SLOTS], dbuf, S_DSUM, DSUM, (row, lax.rem(col + HALF + 1, 2 * HALF))
        )

    def exchange_copies():
        return [
            to(zex.at[peer], ebuf.at[step - 1], S_SWAP, RSUM, (peer, col))
            for step, peer in row_peers()
        ]

    def part_copy():
        return to(pvec, pbuf.at[col - HALF], S_PART, PVEC + col - HALF, (row, HALF))

    @pl.when(col < HALF)
    def _():
        for number in range(SIDE // Q_STEP):
            chunk(number).start()

    @pl.when(col == HALF)
    def _():
        for copy in stage_copies():
            copy.start()
        for half in range(2):
            parts = []
            for i in range(WIDTH // 2):
                held = window[:, half * (WIDTH // 2) + i].astype(F32)
                held = jnp.concatenate([held, jnp.zeros((8 - LINES, SIDE), F32)], axis=0)
                parts.append(jnp.concatenate([held, jnp.zeros((8, 64 - SIDE), F32)], axis=1))
            parts.append(jnp.zeros((8, 64), F32))
            stage[half, BLOCKS - 1] = jnp.concatenate(parts, axis=1).astype(BF16)
        for copy in stage_copies():
            copy.wait()

    @pl.when(col >= HALF)
    def _():
        fetch_density().start()

    greet()

    @pl.when(col < HALF)
    def _():
        own = pieces.at[core, row]
        to(own, own, 0, OWN, (row, HALF)).wait_recv()
        for copy in piece_copies():
            copy.start()
        for (step, source), forward in zip(row_sources(), twin_copies()):
            piece = pieces.at[core, source]
            to(piece, piece, 0, PIECE + step, (source, col)).wait_recv()
            forward.start()
        to(cols.at[0:LINES], cols.at[0:LINES], 0, COLS, (row, HALF)).wait_recv()
        to(trial, ctrial.at[0], 0, CT, (row, HALF)).wait_recv()

        @pl.when(col < HALF - 1)
        def _():
            to(cols.at[LINES:SLOTS], cols.at[LINES:SLOTS], 0, NEXT, (row, HALF)).wait_recv()
            to(trial, ctrial.at[1], 0, CTN, (row, HALF)).wait_recv()

        prepare_columns()
        for source in range(ROWS):
            unpack_piece(core, source)
        other = pieces.at[1 - core]
        to(other, other, 0, TWIN, twin).wait_recv()
        for source in range(ROWS):
            unpack_piece(1 - core, source)
        to(trial, ptrial, 0, PT, (row, HALF)).wait_recv()
        prepare_panel()
        sent = pieces.at[core, 0 : ROWS - 1]
        to(sent, sent, S_PIECE, 0, twin).wait_send()
        sent = pieces.at[core]
        to(sent, sent, S_TWIN, 0, twin).wait_send()

        def one_chunk(number, carry):
            chunk(number).wait()
            for k in range(Q_STEP):
                one_block(number * Q_STEP + k)
            return carry

        lax.fori_loop(0, SIDE // Q_STEP, one_chunk, 0)
        finish()
        for copy in sum_copies():
            copy.start()
        near_sum().start()

        @pl.when(col < HALF - 1)
        def _():
            far_sum().start()

        to(rbuf, rbuf, 0, RSUM, twin).wait_recv()
        total = zrow[row]
        for step in range(ROWS - 1):
            total += rbuf[step]
        ssum[...] = total

    @pl.when(col >= HALF)
    def _():
        @pl.when(col == HALF)
        def _():
            for copy in panel_copies() + trial_copies():
                copy.start()

        fetch_density().wait()

        @pl.when(col == HALF)
        def _():
            row_vectors()
            for copy in vector_copies():
                copy.start()
            rvec[...] = rsend[...]

        @pl.when(col > HALF)
        def _():
            to(rsend, rvec, 0, RVEC, (row, HALF)).wait_recv()
            for copy in next_copies():
                copy.start()

        for copy in column_copies():
            copy.start()

        exchange()
        for copy in exchange_copies():
            copy.start()

        @pl.when(col > HALF)
        def _():
            part_copy().start()

        @pl.when(col == HALF)
        def _():
            for j in range(1, HALF):
                to(pvec, pbuf.at[j], 0, PVEC + j, (row, HALF)).wait_recv()
            exchange_rows()

    @pl.when(col <= HALF)
    def _():
        for copy in final_copies():
            copy.start()
        fbuf[col] = ssum[...]

    @pl.when(col < HALF)
    def _():
        col_part[...] = jnp.zeros_like(col_part)

    @pl.when(col >= HALF)
    def _():
        to(ebuf, ebuf, 0, RSUM, (row, HALF)).wait_recv()
        swapped = zex[row]
        for step in range(ROWS - 1):
            swapped += ebuf[step]
        for copy in column_copies():
            copy.wait_send()
        to(ebuf, ebuf, S_SWAP, 0, twin).wait_send()

        @pl.when(col > HALF)
        def _():
            for copy in next_copies() + [part_copy()]:
                copy.wait_send()

        @pl.when(col == HALF)
        def _():
            to(pieces.at[0], pieces.at[0], S_PANEL, 0, twin).wait_send()
            for copy in trial_copies() + vector_copies():
                copy.wait_send()

        fold = ones_where(iota((128, 128), 0) % 16 == iota((128, 128), 1), F32)
        spots = iota((8, 128), 1) // 16 == iota((8, 128), 0)
        images = []
        for a in range(LINES):
            images.append(dot(jnp.where(spots, swapped[a : a + 1], 0.0), fold, precision=HIGHEST))
        to(zcol.at[0:LINES], cbuf, 0, CSUM, (row, HALF)).wait_recv()

        @pl.when(col > HALF)
        def _():
            to(zcol.at[LINES:SLOTS], dbuf, 0, DSUM, (row, HALF)).wait_recv()

        for a in range(LINES):
            image = images[a] + cbuf[a]
            if a < LINES - 1:
                image += jnp.where(col > HALF, dbuf[a], 0.0)
            col_part[a] = image

    @pl.when(col <= HALF)
    def _():
        to(fbuf.at[0:HALF], fbuf.at[0:HALF], 0, FINAL, twin).wait_recv()

    @pl.when(col > HALF)
    def _():
        to(fbuf.at[0 : HALF + 1], fbuf.at[0 : HALF + 1], 0, FINAL, twin).wait_recv()

    total = fbuf[0]
    for source in range(1, HALF + 1):
        total += fbuf[source]
    row_part[...] = total

    @pl.when(col < HALF)
    def _():
        to(rbuf, rbuf, S_RSUM, 0, twin).wait_send()
        near_sum().wait_send()

        @pl.when(col < HALF - 1)
        def _():
            far_sum().wait_send()

    @pl.when(col <= HALF)
    def _():
        sent = fbuf.at[0 : 2 * HALF - 1]
        to(sent, sent, S_FINAL, 0, twin).wait_send()


def place_kernel(row_part, col_part, row_image, col_image):
    choose = ones_where(
        iota((8, 128), 1) == iota((8, 128), 0) * 16 + lax.axis_index("col"), F32
    )
    picked = dot(choose, row_part[...], (1, 1), HIGHEST)
    for t in range(LINES):
        row_image[t] = picked[t : t + 1, 0:WIDTH]
    for a in range(LINES):
        col_image[a] = col_part[a, 0:WIDTH, 0:16]


def local(band_factors, pair_density, screened, coulomb, window_mask, trial_vector):
    trial = trial_vector.transpose(1, 0, 2)
    vmem = pltpu.VMEM
    parts = pl.pallas_call(
        panel_product_kernel,
        name="panel_product",
        out_shape=[
            jax.ShapeDtypeStruct((8, 128), F32),
            jax.ShapeDtypeStruct((LINES, 8, 128), F32),
        ],
        in_specs=[ANY, ANY, ANY, ANY, VMEM, VMEM, VMEM],
        out_specs=[VMEM, VMEM],
        scratch_shapes=[
            vmem((LINES, SIDE, 256, 256), BF16),
            vmem((LINES, SIDE, 16, 256), BF16),
            vmem((2, BLOCKS, 8, 256), BF16),
            vmem((2, ROWS, BLOCKS, 8, 256), BF16),
            vmem((SLOTS, WIDTH, 8, 256), BF16),
            vmem((2, LINES, 16, SIDE), BF16),
            vmem((LINES, 16, SIDE), BF16),
            vmem((LINES, 8, 256), F32),
            vmem((LINES, 8, 256), F32),
            vmem((2, LINES * 8 * SIDE, 128), F32),
            vmem((2, LINES * 4 * RING, 128), F32),
            vmem((2, LINES * 4 * RING, 128), F32),
            vmem((LINES * LINES * RING, 128), F32),
            vmem((2, LINES * 4 * RING, 128), F32),
            vmem((2, SLOTS * 64, 128), F32),
            vmem((SLOTS * 32, 256), BF16),
            vmem((2, SLOTS * 32, 128), F32),
            vmem((2, SLOTS * 32, 128), F32),
            vmem((ROWS, 8, 128), F32),
            vmem((SLOTS, 8, 128), F32),
            vmem((LINES, 8, 256), F32),
            vmem((ROWS, 8, 128), F32),
            vmem((ROWS - 1, 8, 128), F32),
            vmem((LINES, 8, 128), F32),
            vmem((SLOTS - LINES, 8, 128), F32),
            vmem((HALF, LINES, 8, 256), F32),
            vmem((ROWS - 1, 8, 128), F32),
            vmem((2 * HALF, 8, 128), F32),
            vmem((8, 128), F32),
            pltpu.SemaphoreType.DMA((29,)),
            pltpu.SemaphoreType.DMA((28,)),
            pltpu.SemaphoreType.DMA((7,)),
            pltpu.SemaphoreType.DMA((SIDE // Q_STEP,)),
        ],
        compiler_params=pltpu.CompilerParams(
            collective_id=0, has_side_effects=True, vmem_limit_bytes=56 * 1024 * 1024
        ),
    )(
        band_factors,
        pair_density,
        screened,
        trial,
        window_mask,
        trial,
        coulomb.reshape(1, 256),
    )
    row_image, col_image = pl.pallas_call(
        place_kernel,
        name="place",
        out_shape=[
            jax.ShapeDtypeStruct((LINES, 1, WIDTH), F32),
            jax.ShapeDtypeStruct((LINES, WIDTH, 16), F32),
        ],
        in_specs=[VMEM, VMEM],
        out_specs=[VMEM, VMEM],
    )(*parts)
    return row_image.transpose(1, 0, 2), col_image.transpose(2, 0, 1)


def solution(mesh):
    placed = (
        P("col", None, None, None),
        P("col", None, None, None),
        P("col", None, None, None),
        P(),
        P(None, "row", None),
        P(None, "col", None),
    )
    return jax.shard_map(
        local,
        mesh=mesh,
        in_specs=placed,
        out_specs=(P("col", None, "row"), P(None, "col", "row")),
        check_vma=False,
    )
```

```python
import functools

import jax
import jax.numpy as jnp
from jax import lax
from jax.experimental import pallas as pl
from jax.experimental.pallas import tpu as pltpu
from jax.sharding import PartitionSpec as P

MESH = pl.DeviceIdType.MESH
F32 = jnp.float32
BF16 = jnp.bfloat16
SIDE = 48
ROWS = 8
WIDTH = 6
LINES = 3
HALF = 8
SLOTS = 2 * LINES - 1
RING = SIDE + 8
BLOCKS = LINES * WIDTH // 2 + 1
Q_STEP = 4
HIGHEST = lax.Precision.HIGHEST
ANY = pl.BlockSpec(memory_space=pl.ANY)
VMEM = pl.BlockSpec(memory_space=pltpu.VMEM)


def iota(shape, axis):
    return lax.broadcasted_iota(jnp.int32, shape, axis)


def dot(a, b, contract=(1, 0), precision=None):
    return lax.dot_general(
        a,
        b,
        (((contract[0],), (contract[1],)), ((), ())),
        preferred_element_type=F32,
        precision=precision,
    )


def ones_where(condition, dtype=BF16):
    return jnp.where(condition, 1.0, 0.0).astype(dtype)


def pick_rows(trial_line, first):
    pick = ones_where(iota((8, SIDE), 1) == first + iota((8, SIDE), 0))
    return dot(pick, trial_line, (1, 1)).astype(BF16)


def block_diagonal(trial_line, first, copies):
    rows = pick_rows(trial_line, first)
    tiled = dot(rows, ones_where(iota((16, copies * 16), 1) % 16 == iota((16, copies * 16), 0)))
    return jnp.where(iota(tiled.shape, 1) // 16 == iota(tiled.shape, 0), tiled, 0.0)


def greet():
    row, col = lax.axis_index("row"), lax.axis_index("col")
    barrier = pltpu.get_barrier_semaphore()
    for step in range(1, ROWS):
        pl.semaphore_signal(
            barrier, inc=1, device_id=(lax.rem(row + step, ROWS), col), device_id_type=MESH
        )
    for step in range(1, 2 * HALF):
        pl.semaphore_signal(
            barrier, inc=1, device_id=(row, lax.rem(col + step, 2 * HALF)), device_id_type=MESH
        )
    pl.semaphore_wait(barrier, ROWS + 2 * HALF - 2)


def remote(source, target, send_sem, recv_sem, device):
    return pltpu.make_async_remote_copy(
        src_ref=source,
        dst_ref=target,
        send_sem=send_sem,
        recv_sem=recv_sem,
        device_id=device,
        device_id_type=MESH,
    )


def panel_product_kernel(
    bands,
    density,
    blocks,
    trial,
    window,
    trial_v,
    coulomb,
    row_part,
    col_part,
    w_buf,
    dens,
    stage,
    pieces,
    cols,
    ctrial,
    ptrial,
    rsend,
    rvec,
    flat,
    left_t,
    y_row,
    keep_t,
    r_sum,
    col_flat,
    u_col,
    y_col,
    c_sum,
    zrow,
    zcol,
    pvec,
    zex,
    rbuf,
    cbuf,
    dbuf,
    pbuf,
    ebuf,
    fbuf,
    ssum,
    send,
    recv,
    local,
    w_sem,
):
    row, col = lax.axis_index("row"), lax.axis_index("col")
    first = row * WIDTH
    core = lax.rem(col, 2)
    twin = (row, col + 1 - 2 * core)
    halves = (slice(0, 128), slice(128, 256))
    spread = ones_where(iota((16, 2048), 1) // 128 == iota((16, 2048), 0))

    def to(source, target, number, arrives, device):
        return remote(source, target, send.at[number], recv.at[arrives], device)

    def row_peers():
        return [(step, lax.rem(row + step, ROWS)) for step in (5, 3, 7, 1, 4, 2, 6)]

    def row_sources():
        return [(step, lax.rem(row + ROWS - step, ROWS)) for step in (2, 6, 4, 1, 7, 3, 5)]

    COLS, NEXT, CT, CTN, PT, OWN, RVEC, TWIN, PIECE = 0, 1, 2, 3, 4, 5, 6, 7, 8
    RSUM, CSUM, DSUM, FINAL, PVEC = 16, 17, 18, 19, 20
    S_PIECE, S_TWIN, S_RSUM, S_CSUM, S_DSUM, S_FINAL, S_SWAP = 0, 1, 2, 3, 4, 5, 6
    S_PANEL, S_TRIAL, S_VECTOR, S_PART, S_COLUMN = 7, 8, 16, 24, 25

    def lane(expanded, s):
        return expanded[:, s * 128 : (s + 1) * 128]

    def chunk(number):
        return pltpu.make_async_copy(
            blocks.at[:, pl.ds(number * Q_STEP, Q_STEP)],
            w_buf.at[:, pl.ds(number * Q_STEP, Q_STEP)],
            w_sem.at[number],
        )

    def stage_copies():
        copies = []
        for half in range(2):
            for t in range(LINES):
                source = bands.at[t, pl.ds(first + half * (WIDTH // 2), WIDTH // 2)]
                number = half * LINES + t
                place = stage.at[half, pl.ds(t * (WIDTH // 2), WIDTH // 2)]
                copies.append(pltpu.make_async_copy(source, place, local.at[1 + number]))
        return copies

    def fetch_density():
        return pltpu.make_async_copy(density, dens, local.at[0])

    def store_ring(table, h, number, value):
        base = number * RING
        table[h, base : base + SIDE, :] = value
        table[h, base + SIDE : base + RING, :] = value[0:8]

    def unpack_piece(half, source):
        for t in range(LINES):
            lines = slice(t * (WIDTH // 2), (t + 1) * (WIDTH // 2))
            value = pieces[half, source, lines].astype(F32).reshape(WIDTH * 4, 256)
            base = pl.multiple_of((t * SIDE + source * WIDTH + half * (WIDTH // 2)) * 8, 8)
            for h in range(2):
                flat[h, pl.ds(base, WIDTH * 4), :] = value[:, halves[h]]

    def prepare_panel():
        for t in range(LINES):
            line = jnp.transpose(ptrial[t].astype(F32)).astype(BF16)
            expanded = dot(line, spread)
            for h in range(2):

                def band(number):
                    return flat[h, pl.ds(t * 8 * SIDE + number, SIDE, stride=8), :]

                for c in range(4):
                    store_ring(left_t, h, t * 4 + c, band(c))
                valence = [band(4 + v) for v in range(4)]
                for c in range(4):
                    total = valence[0] * lane(expanded, c)
                    for v in range(1, 4):
                        total += valence[v] * lane(expanded, 4 * v + c)
                    store_ring(y_row, h, t * 4 + c, total)
        places = iota((8, 256), 1)
        rows = iota((8, 256), 0)
        for e in range(LINES):
            line = HALF * LINES + col * LINES + e + rows
            for source in range(ROWS):
                for half in range(2):
                    wide = pieces[half, source, BLOCKS - 1].astype(F32)
                    for i in range(WIDTH // 2):
                        held = jnp.where((places == line + 64 * i) & (rows < LINES), wide, 0.0)
                        factor = jnp.sum(held, axis=1, keepdims=True)
                        factor = jnp.broadcast_to(factor, (8, 128))
                        b = source * WIDTH + half * (WIDTH // 2) + i
                        for t in range(LINES):
                            base = (e * LINES + t) * RING
                            keep_t[base + b : base + b + 1, :] = factor[t : t + 1]
                            if b < 8:
                                base += SIDE
                                keep_t[base + b : base + b + 1, :] = factor[t : t + 1]
        r_sum[...] = jnp.zeros_like(r_sum)

    def prepare_columns():
        for a in range(SLOTS):
            value = cols[a].astype(F32).reshape(WIDTH * 8, 256)
            if a >= LINES:
                value = jnp.where(col < HALF - 1, value, 0.0)
            for h in range(2):
                col_flat[h, a * 64 : a * 64 + WIDTH * 8, :] = value[:, halves[h]]
                col_flat[h, a * 64 + WIDTH * 8 : a * 64 + 64, :] = jnp.zeros((16, 128), F32)
        for a in range(SLOTS):
            line = ctrial[a // LINES, a % LINES]
            expanded = dot(pick_rows(line, first), spread)
            if a >= LINES:
                expanded = jnp.where(col < HALF - 1, expanded, 0.0)
            for h in range(2):

                def band(number):
                    return col_flat[h, pl.ds(a * 64 + number, 8, stride=8), :]

                for pair in range(2):
                    both = jnp.concatenate([band(2 * pair), band(2 * pair + 1)], axis=0)
                    u_col[a * 32 + pair * 16 : a * 32 + pair * 16 + 16, halves[h]] = both.astype(
                        BF16
                    )
                valence = [band(4 + v) for v in range(4)]
                for c in range(4):
                    total = valence[0] * lane(expanded, c)
                    for v in range(1, 4):
                        total += valence[v] * lane(expanded, 4 * v + c)
                    y_col[h, (a * 4 + c) * 8 : (a * 4 + c) * 8 + 8, :] = total
        c_sum[...] = jnp.zeros_like(c_sum)

    def one_block(q_value):
        start = lax.rem(first + SIDE - q_value, SIDE)
        inside = (first + iota((8, 128), 0) >= q_value) | (col > 0)
        same = (q_value == 0) & (col == 0)

        def rows(table, t, c, h):
            return table[h, pl.ds((t * 4 + c) * RING + start, 8), :]

        for e in range(LINES):
            tiles = []
            for t in range(LINES):
                a = t + e
                factor = keep_t[pl.ds((e * LINES + t) * RING + start, 8), :]
                if e == 0:
                    factor = jnp.where(inside, factor, 0.0)
                for c in range(4):
                    both = []
                    for h in range(2):
                        kept = rows(left_t, t, c, h) * factor
                        both.append(jnp.concatenate([kept, kept], axis=0).astype(BF16))
                    both = jnp.concatenate(both, axis=1)
                    for pair in range(2):
                        base = a * 32 + pair * 16
                        tiles.append(both * u_col[base : base + 16, :])
            mixed = dot(jnp.concatenate(tiles, axis=0), w_buf[e, q_value])
            for t in range(LINES):
                a = t + e
                for h in range(2):
                    images = [None] * 4
                    for c in range(4):
                        total = None
                        back = rows(y_row, t, c, h)
                        for d in range(4):
                            base = t * 128 + (c * 4 + d) * 8
                            piece = mixed[base : base + 8, halves[h]]
                            base = (a * 4 + d) * 8
                            part = piece * y_col[h, base : base + 8, :]
                            total = part if total is None else total + part
                            part = piece * back
                            images[d] = part if images[d] is None else images[d] + part
                        r_sum[h, pl.ds((t * 4 + c) * RING + start, 8), :] += total
                    for d in range(4):
                        base = (a * 4 + d) * 8
                        image = jnp.where(same, 0.0, images[d]) if e == 0 else images[d]
                        c_sum[h, base : base + 8, :] += image

    def finish():
        lanes = iota((SIDE, 128), 1)
        image = jnp.zeros((SIDE, 128), F32)
        for t in range(LINES):
            for c in range(4):
                base = (t * 4 + c) * RING
                total = []
                for h in range(2):
                    head = r_sum[h, base : base + 8, :] + r_sum[h, base + SIDE : base + RING, :]
                    total.append(
                        jnp.concatenate([head, r_sum[h, base + 8 : base + SIDE, :]], axis=0)
                    )
                for v in range(4):
                    product = 0.0
                    for h in range(2):
                        strided = pl.ds(t * 8 * SIDE + 4 + v, SIDE, stride=8)
                        product += flat[h, strided, :] * total[h]
                    value = jnp.sum(product, axis=1, keepdims=True)
                    image = jnp.where(lanes == t * 16 + 4 * v + c, value, image)
        for target in range(ROWS):
            zrow[target, 0:WIDTH, :] = -image[target * WIDTH : (target + 1) * WIDTH]
            zrow[target, WIDTH:8, :] = jnp.zeros((8 - WIDTH, 128), F32)
        lanes = iota((8, 128), 1)
        for a in range(SLOTS):
            image = jnp.zeros((8, 128), F32)
            for v in range(4):
                for c in range(4):
                    product = 0.0
                    for h in range(2):
                        base = (a * 4 + c) * 8
                        strided = pl.ds(a * 64 + 4 + v, 8, stride=8)
                        product += col_flat[h, strided, :] * c_sum[h, base : base + 8, :]
                    value = jnp.sum(product, axis=1, keepdims=True)
                    image = jnp.where(lanes == 4 * v + c, value, image)
            zcol[a] = -image

    def exchange():
        tile = ones_where(iota((16, SIDE * 16), 1) % 16 == iota((16, SIDE * 16), 0))
        own_point = iota((SIDE, SIDE * 16), 1) // 16 == iota((SIDE, SIDE * 16), 0)
        ones = jnp.ones((8, SIDE), BF16)
        points = iota((8, SIDE * 16), 1) // 16
        row_points = first + iota((8, SIDE * 16), 0)
        places = iota((WIDTH, SIDE), 1)
        wide = jnp.concatenate([rvec[t] for t in range(LINES)], axis=0)
        high = wide.astype(BF16)
        low = (wide - high.astype(F32)).astype(BF16)
        split = jnp.concatenate([high, low], axis=0)
        zex[...] = jnp.zeros_like(zex)
        sums = jnp.zeros((8 * LINES, 256), F32)
        for a in range(LINES):
            line = col * LINES + a
            transposed = jnp.transpose(trial_v[a].astype(F32)).astype(BF16)
            values = jnp.where(own_point, dot(transposed, tile), 0.0).astype(BF16)
            values = dot(ones, values)
            kept_values = []
            strict_factors = []
            for t in range(LINES):
                row_line = HALF * LINES + t
                held = jnp.where(places == line, window[t], 0).astype(F32)
                held = jnp.sum(held, axis=1, keepdims=True)
                held = jnp.concatenate([held, jnp.zeros((8 - WIDTH, 1), F32)], axis=0)
                kept = (line > row_line) | ((line == row_line) & (points >= row_points))
                strict = (line > row_line) | ((line == row_line) & (points > row_points))
                kept_values.append(jnp.where(kept, held, 0.0) * values)
                strict_factors.append(jnp.where(strict, held, 0.0))
            table = dens[a].reshape(SIDE * 16, 256)
            sums += dot(jnp.concatenate(kept_values, axis=0).astype(BF16), table)
            products = dot(split, table, (1, 1))
            products = products[0 : 8 * LINES] + products[8 * LINES : 16 * LINES]
            image = jnp.sum(
                products * jnp.concatenate(strict_factors, axis=0), axis=0, keepdims=True
            )
            for target in range(ROWS):
                lanes = slice(target * WIDTH * 16, (target + 1) * WIDTH * 16)
                zex[target, a : a + 1, 0 : WIDTH * 16] = 2.0 * image[:, lanes]
        for t in range(LINES):
            pvec[t] = sums[t * 8 : t * 8 + 8]

    def row_vectors():
        for t in range(LINES):
            diagonal = block_diagonal(trial_v[t], first, WIDTH).astype(BF16)
            scaled = (dens[t, pl.ds(first, WIDTH)].astype(F32) * coulomb[...]).astype(BF16)
            rsend[t] = dot(diagonal, scaled.reshape(WIDTH * 16, 256))

    def exchange_rows():
        total = jnp.zeros((8, 128), F32)
        lanes = WIDTH * 16
        own = iota((8, lanes), 1) // 16 == iota((8, lanes), 0)
        for t in range(LINES):
            summed = pvec[t]
            for j in range(1, HALF):
                summed += pbuf[j, t]
            scaled = (dens[t, pl.ds(first, WIDTH)].astype(F32) * coulomb[...]).astype(BF16)
            scaled = scaled.reshape(lanes, 256)
            high = summed.astype(BF16)
            low = (summed - high.astype(F32)).astype(BF16)
            products = dot(jnp.concatenate([high, low], axis=0), scaled, (1, 1))
            products = jnp.where(own, products[0:8] + products[8:16], 0.0)
            fold = ones_where(iota((lanes, 128), 0) % 16 + t * 16 == iota((lanes, 128), 1), F32)
            total += dot(products, fold, precision=HIGHEST)
        ssum[...] = 2.0 * total

    def final_copies():
        copies = []
        for step in (8, 9, 10, 11, 7, 6, 5, 4, 12, 13, 14, 15, 3, 2, 1):
            peer = lax.rem(col + step, 2 * HALF)
            copies.append(to(ssum, fbuf.at[col], S_FINAL, FINAL, (row, peer)))
        return copies

    def panel_copies():
        return [to(stage.at[j % 2], pieces.at[j % 2, row], S_PANEL, OWN, (row, j)) for j in range(HALF)]

    def trial_copies():
        return [to(trial, ptrial, S_TRIAL + j, PT, (row, j)) for j in range(HALF)]

    def column_copies():
        near = (row, lax.rem(col + HALF, 2 * HALF))
        own = bands.at[:, pl.ds(first, WIDTH)]
        return [
            to(own, cols.at[0:LINES], S_COLUMN, COLS, near),
            to(trial, ctrial.at[0], S_COLUMN + 1, CT, near),
        ]

    def next_copies():
        far = (row, lax.rem(col + HALF - 1, 2 * HALF))
        own = bands.at[0 : LINES - 1, pl.ds(first, WIDTH)]
        return [
            to(own, cols.at[LINES:SLOTS], S_COLUMN + 2, NEXT, far),
            to(trial, ctrial.at[1], S_COLUMN + 3, CTN, far),
        ]

    def vector_copies():
        return [to(rsend, rvec, S_VECTOR + j, RVEC, (row, HALF + j)) for j in range(1, HALF)]

    def piece_copies():
        own = pieces.at[core, row]
        return [
            to(own, own, S_PIECE, PIECE + step, (peer, col)) for step, peer in row_peers()
        ] + [to(own, own, S_TWIN, TWIN, twin)]

    def twin_copies():
        return [
            to(pieces.at[core, source], pieces.at[core, source], S_TWIN, TWIN, twin)
            for step, source in row_sources()
        ]

    def sum_copies():
        return [
            to(zrow.at[peer], rbuf.at[step - 1], S_RSUM, RSUM, (peer, col))
            for step, peer in row_peers()
        ]

    def near_sum():
        return to(zcol.at[0:LINES], cbuf, S_CSUM, CSUM, (row, lax.rem(col + HALF, 2 * HALF)))

    def far_sum():
        return to(
            zcol.at[LINES:SLOTS], dbuf, S_DSUM, DSUM, (row, lax.rem(col + HALF + 1, 2 * HALF))
        )

    def exchange_copies():
        return [
            to(zex.at[peer], ebuf.at[step - 1], S_SWAP, RSUM, (peer, col))
            for step, peer in row_peers()
        ]

    def part_copy():
        return to(pvec, pbuf.at[col - HALF], S_PART, PVEC + col - HALF, (row, HALF))

    @pl.when(col < HALF)
    def _():
        for number in range(SIDE // Q_STEP):
            chunk(number).start()

    @pl.when(col == HALF)
    def _():
        for copy in stage_copies():
            copy.start()
        for half in range(2):
            parts = []
            for i in range(WIDTH // 2):
                held = window[:, half * (WIDTH // 2) + i].astype(F32)
                held = jnp.concatenate([held, jnp.zeros((8 - LINES, SIDE), F32)], axis=0)
                parts.append(jnp.concatenate([held, jnp.zeros((8, 64 - SIDE), F32)], axis=1))
            parts.append(jnp.zeros((8, 64), F32))
            stage[half, BLOCKS - 1] = jnp.concatenate(parts, axis=1).astype(BF16)
        for copy in stage_copies():
            copy.wait()

    @pl.when(col >= HALF)
    def _():
        fetch_density().start()

    greet()

    @pl.when(col < HALF)
    def _():
        own = pieces.at[core, row]
        to(own, own, 0, OWN, (row, HALF)).wait_recv()
        for copy in piece_copies():
            copy.start()
        for (step, source), forward in zip(row_sources(), twin_copies()):
            piece = pieces.at[core, source]
            to(piece, piece, 0, PIECE + step, (source, col)).wait_recv()
            forward.start()
        to(cols.at[0:LINES], cols.at[0:LINES], 0, COLS, (row, HALF)).wait_recv()
        to(trial, ctrial.at[0], 0, CT, (row, HALF)).wait_recv()

        @pl.when(col < HALF - 1)
        def _():
            to(cols.at[LINES:SLOTS], cols.at[LINES:SLOTS], 0, NEXT, (row, HALF)).wait_recv()
            to(trial, ctrial.at[1], 0, CTN, (row, HALF)).wait_recv()

        prepare_columns()
        for source in range(ROWS):
            unpack_piece(core, source)
        other = pieces.at[1 - core]
        to(other, other, 0, TWIN, twin).wait_recv()
        for source in range(ROWS):
            unpack_piece(1 - core, source)
        to(trial, ptrial, 0, PT, (row, HALF)).wait_recv()
        prepare_panel()
        sent = pieces.at[core, 0 : ROWS - 1]
        to(sent, sent, S_PIECE, 0, twin).wait_send()
        sent = pieces.at[core]
        to(sent, sent, S_TWIN, 0, twin).wait_send()

        def one_chunk(number, carry):
            chunk(number).wait()
            for k in range(Q_STEP):
                one_block(number * Q_STEP + k)
            return carry

        lax.fori_loop(0, SIDE // Q_STEP, one_chunk, 0)
        finish()
        for copy in sum_copies():
            copy.start()
        near_sum().start()

        @pl.when(col < HALF - 1)
        def _():
            far_sum().start()

        to(rbuf, rbuf, 0, RSUM, twin).wait_recv()
        total = zrow[row]
        for step in range(ROWS - 1):
            total += rbuf[step]
        ssum[...] = total

    @pl.when(col >= HALF)
    def _():
        @pl.when(col == HALF)
        def _():
            for copy in panel_copies():
                copy.start()

        for copy in column_copies():
            copy.start()

        @pl.when(col > HALF)
        def _():
            for copy in next_copies():
                copy.start()

        fetch_density().wait()

        @pl.when(col == HALF)
        def _():
            for copy in trial_copies():
                copy.start()
            row_vectors()
            for copy in vector_copies():
                copy.start()
            rvec[...] = rsend[...]

        @pl.when(col > HALF)
        def _():
            to(rsend, rvec, 0, RVEC, (row, HALF)).wait_recv()

        exchange()
        for copy in exchange_copies():
            copy.start()

        @pl.when(col > HALF)
        def _():
            part_copy().start()

        @pl.when(col == HALF)
        def _():
            for j in range(1, HALF):
                to(pvec, pbuf.at[j], 0, PVEC + j, (row, HALF)).wait_recv()
            exchange_rows()

    @pl.when(col <= HALF)
    def _():
        for copy in final_copies():
            copy.start()
        fbuf[col] = ssum[...]

    @pl.when(col < HALF)
    def _():
        col_part[...] = jnp.zeros_like(col_part)

    @pl.when(col >= HALF)
    def _():
        to(ebuf, ebuf, 0, RSUM, (row, HALF)).wait_recv()
        swapped = zex[row]
        for step in range(ROWS - 1):
            swapped += ebuf[step]
        for copy in column_copies():
            copy.wait_send()
        to(ebuf, ebuf, S_SWAP, 0, twin).wait_send()

        @pl.when(col > HALF)
        def _():
            for copy in next_copies() + [part_copy()]:
                copy.wait_send()

        @pl.when(col == HALF)
        def _():
            to(pieces.at[0], pieces.at[0], S_PANEL, 0, twin).wait_send()
            for copy in trial_copies() + vector_copies():
                copy.wait_send()

        fold = ones_where(iota((128, 128), 0) % 16 == iota((128, 128), 1), F32)
        spots = iota((8, 128), 1) // 16 == iota((8, 128), 0)
        images = []
        for a in range(LINES):
            images.append(dot(jnp.where(spots, swapped[a : a + 1], 0.0), fold, precision=HIGHEST))
        to(zcol.at[0:LINES], cbuf, 0, CSUM, (row, HALF)).wait_recv()

        @pl.when(col > HALF)
        def _():
            to(zcol.at[LINES:SLOTS], dbuf, 0, DSUM, (row, HALF)).wait_recv()

        for a in range(LINES):
            image = images[a] + cbuf[a]
            if a < LINES - 1:
                image += jnp.where(col > HALF, dbuf[a], 0.0)
            col_part[a] = image

    @pl.when(col <= HALF)
    def _():
        to(fbuf.at[0:HALF], fbuf.at[0:HALF], 0, FINAL, twin).wait_recv()

    @pl.when(col > HALF)
    def _():
        to(fbuf.at[0 : HALF + 1], fbuf.at[0 : HALF + 1], 0, FINAL, twin).wait_recv()

    total = fbuf[0]
    for source in range(1, HALF + 1):
        total += fbuf[source]
    row_part[...] = total

    @pl.when(col < HALF)
    def _():
        to(rbuf, rbuf, S_RSUM, 0, twin).wait_send()
        near_sum().wait_send()

        @pl.when(col < HALF - 1)
        def _():
            far_sum().wait_send()

    @pl.when(col <= HALF)
    def _():
        sent = fbuf.at[0 : 2 * HALF - 1]
        to(sent, sent, S_FINAL, 0, twin).wait_send()


def place_kernel(row_part, col_part, row_image, col_image):
    choose = ones_where(
        iota((8, 128), 1) == iota((8, 128), 0) * 16 + lax.axis_index("col"), F32
    )
    picked = dot(choose, row_part[...], (1, 1), HIGHEST)
    for t in range(LINES):
        row_image[t] = picked[t : t + 1, 0:WIDTH]
    for a in range(LINES):
        col_image[a] = col_part[a, 0:WIDTH, 0:16]


def local(band_factors, pair_density, screened, coulomb, window_mask, trial_vector):
    trial = trial_vector.transpose(1, 0, 2)
    vmem = pltpu.VMEM
    parts = pl.pallas_call(
        panel_product_kernel,
        name="panel_product",
        out_shape=[
            jax.ShapeDtypeStruct((8, 128), F32),
            jax.ShapeDtypeStruct((LINES, 8, 128), F32),
        ],
        in_specs=[ANY, ANY, ANY, ANY, VMEM, VMEM, VMEM],
        out_specs=[VMEM, VMEM],
        scratch_shapes=[
            vmem((LINES, SIDE, 256, 256), BF16),
            vmem((LINES, SIDE, 16, 256), BF16),
            vmem((2, BLOCKS, 8, 256), BF16),
            vmem((2, ROWS, BLOCKS, 8, 256), BF16),
            vmem((SLOTS, WIDTH, 8, 256), BF16),
            vmem((2, LINES, 16, SIDE), BF16),
            vmem((LINES, 16, SIDE), BF16),
            vmem((LINES, 8, 256), F32),
            vmem((LINES, 8, 256), F32),
            vmem((2, LINES * 8 * SIDE, 128), F32),
            vmem((2, LINES * 4 * RING, 128), F32),
            vmem((2, LINES * 4 * RING, 128), F32),
            vmem((LINES * LINES * RING, 128), F32),
            vmem((2, LINES * 4 * RING, 128), F32),
            vmem((2, SLOTS * 64, 128), F32),
            vmem((SLOTS * 32, 256), BF16),
            vmem((2, SLOTS * 32, 128), F32),
            vmem((2, SLOTS * 32, 128), F32),
            vmem((ROWS, 8, 128), F32),
            vmem((SLOTS, 8, 128), F32),
            vmem((LINES, 8, 256), F32),
            vmem((ROWS, 8, 128), F32),
            vmem((ROWS - 1, 8, 128), F32),
            vmem((LINES, 8, 128), F32),
            vmem((SLOTS - LINES, 8, 128), F32),
            vmem((HALF, LINES, 8, 256), F32),
            vmem((ROWS - 1, 8, 128), F32),
            vmem((2 * HALF, 8, 128), F32),
            vmem((8, 128), F32),
            pltpu.SemaphoreType.DMA((29,)),
            pltpu.SemaphoreType.DMA((28,)),
            pltpu.SemaphoreType.DMA((7,)),
            pltpu.SemaphoreType.DMA((SIDE // Q_STEP,)),
        ],
        compiler_params=pltpu.CompilerParams(
            collective_id=0, has_side_effects=True, vmem_limit_bytes=56 * 1024 * 1024
        ),
    )(
        band_factors,
        pair_density,
        screened,
        trial,
        window_mask,
        trial,
        coulomb.reshape(1, 256),
    )
    row_image, col_image = pl.pallas_call(
        place_kernel,
        name="place",
        out_shape=[
            jax.ShapeDtypeStruct((LINES, 1, WIDTH), F32),
            jax.ShapeDtypeStruct((LINES, WIDTH, 16), F32),
        ],
        in_specs=[VMEM, VMEM],
        out_specs=[VMEM, VMEM],
    )(*parts)
    return row_image.transpose(1, 0, 2), col_image.transpose(2, 0, 1)


def solution(mesh):
    placed = (
        P("col", None, None, None),
        P("col", None, None, None),
        P("col", None, None, None),
        P(),
        P(None, "row", None),
        P(None, "col", None),
    )
    return jax.shard_map(
        local,
        mesh=mesh,
        in_specs=placed,
        out_specs=(P("col", None, "row"), P(None, "col", "row")),
        check_vma=False,
    )
```

```python
import functools

import jax
import jax.numpy as jnp
from jax import lax
from jax.experimental import pallas as pl
from jax.experimental.pallas import tpu as pltpu
from jax.sharding import PartitionSpec as P

MESH = pl.DeviceIdType.MESH
F32 = jnp.float32
BF16 = jnp.bfloat16
SIDE = 48
ROWS = 8
WIDTH = 6
LINES = 3
HALF = 8
SLOTS = 2 * LINES - 1
RING = SIDE + 8
BLOCKS = LINES * WIDTH // 2 + 1
Q_STEP = 4
HIGHEST = lax.Precision.HIGHEST
ANY = pl.BlockSpec(memory_space=pl.ANY)
VMEM = pl.BlockSpec(memory_space=pltpu.VMEM)


def iota(shape, axis):
    return lax.broadcasted_iota(jnp.int32, shape, axis)


def dot(a, b, contract=(1, 0), precision=None):
    return lax.dot_general(
        a,
        b,
        (((contract[0],), (contract[1],)), ((), ())),
        preferred_element_type=F32,
        precision=precision,
    )


def ones_where(condition, dtype=BF16):
    return jnp.where(condition, 1.0, 0.0).astype(dtype)


def pick_rows(trial_line, first):
    pick = ones_where(iota((8, SIDE), 1) == first + iota((8, SIDE), 0))
    return dot(pick, trial_line, (1, 1)).astype(BF16)


def block_diagonal(trial_line, first, copies):
    rows = pick_rows(trial_line, first)
    tiled = dot(rows, ones_where(iota((16, copies * 16), 1) % 16 == iota((16, copies * 16), 0)))
    return jnp.where(iota(tiled.shape, 1) // 16 == iota(tiled.shape, 0), tiled, 0.0)


def greet():
    row, col = lax.axis_index("row"), lax.axis_index("col")
    barrier = pltpu.get_barrier_semaphore()
    for step in range(1, ROWS):
        pl.semaphore_signal(
            barrier, inc=1, device_id=(lax.rem(row + step, ROWS), col), device_id_type=MESH
        )
    for step in range(1, 2 * HALF):
        pl.semaphore_signal(
            barrier, inc=1, device_id=(row, lax.rem(col + step, 2 * HALF)), device_id_type=MESH
        )


def remote(source, target, send_sem, recv_sem, device):
    return pltpu.make_async_remote_copy(
        src_ref=source,
        dst_ref=target,
        send_sem=send_sem,
        recv_sem=recv_sem,
        device_id=device,
        device_id_type=MESH,
    )


def panel_product_kernel(
    bands,
    density,
    blocks,
    trial,
    window,
    trial_v,
    coulomb,
    row_part,
    col_part,
    w_buf,
    dens,
    stage,
    pieces,
    cols,
    ctrial,
    ptrial,
    rsend,
    rvec,
    flat,
    left_t,
    y_row,
    keep_t,
    r_sum,
    col_flat,
    u_col,
    y_pair,
    c_sum,
    zrow,
    zcol,
    pvec,
    zex,
    rbuf,
    cbuf,
    dbuf,
    pbuf,
    ebuf,
    fbuf,
    ssum,
    send,
    recv,
    local,
    w_sem,
):
    row, col = lax.axis_index("row"), lax.axis_index("col")
    first = row * WIDTH
    core = lax.rem(col, 2)
    twin = (row, col + 1 - 2 * core)
    halves = (slice(0, 128), slice(128, 256))
    spread = ones_where(iota((16, 2048), 1) // 128 == iota((16, 2048), 0))

    def to(source, target, number, arrives, device):
        return remote(source, target, send.at[number], recv.at[arrives], device)

    def row_peers():
        return [(step, lax.rem(row + step, ROWS)) for step in (5, 3, 7, 1, 4, 2, 6)]

    def row_sources():
        return [(step, lax.rem(row + ROWS - step, ROWS)) for step in (2, 6, 4, 1, 7, 3, 5)]

    COLS, NEXT, CT, CTN, PT, OWN, RVEC, TWIN, PIECE = 0, 1, 2, 3, 4, 5, 6, 7, 8
    RSUM, CSUM, DSUM, FINAL, PVEC = 16, 17, 18, 19, 20
    S_PIECE, S_TWIN, S_RSUM, S_CSUM, S_DSUM, S_FINAL, S_SWAP = 0, 1, 2, 3, 4, 5, 6
    S_PANEL, S_TRIAL, S_VECTOR, S_PART, S_COLUMN = 7, 8, 16, 24, 25

    def lane(expanded, s):
        return expanded[:, s * 128 : (s + 1) * 128]

    def chunk(number):
        return pltpu.make_async_copy(
            blocks.at[:, pl.ds(number * Q_STEP, Q_STEP)],
            w_buf.at[:, pl.ds(number * Q_STEP, Q_STEP)],
            w_sem.at[number],
        )

    def stage_copies():
        copies = []
        for half in range(2):
            for t in range(LINES):
                source = bands.at[t, pl.ds(first + half * (WIDTH // 2), WIDTH // 2)]
                number = half * LINES + t
                place = stage.at[half, pl.ds(t * (WIDTH // 2), WIDTH // 2)]
                copies.append(pltpu.make_async_copy(source, place, local.at[1 + number]))
        return copies

    def fetch_density():
        return pltpu.make_async_copy(density, dens, local.at[0])

    def store_ring(table, h, number, value):
        base = number * RING
        table[h, base : base + SIDE, :] = value
        table[h, base + SIDE : base + RING, :] = value[0:8]

    def unpack_piece(half, source):
        for t in range(LINES):
            lines = slice(t * (WIDTH // 2), (t + 1) * (WIDTH // 2))
            value = pieces[half, source, lines].astype(F32).reshape(WIDTH * 4, 256)
            base = pl.multiple_of((t * SIDE + source * WIDTH + half * (WIDTH // 2)) * 8, 8)
            for h in range(2):
                flat[h, pl.ds(base, WIDTH * 4), :] = value[:, halves[h]]

    def prepare_panel():
        for t in range(LINES):
            line = jnp.transpose(ptrial[t].astype(F32)).astype(BF16)
            expanded = dot(line, spread)
            for h in range(2):

                def band(number):
                    return flat[h, pl.ds(t * 8 * SIDE + number, SIDE, stride=8), :]

                for c in range(4):
                    store_ring(left_t, h, t * 4 + c, band(c))
                valence = [band(4 + v) for v in range(4)]
                for c in range(4):
                    total = valence[0] * lane(expanded, c)
                    for v in range(1, 4):
                        total += valence[v] * lane(expanded, 4 * v + c)
                    store_ring(y_row, h, t * 4 + c, total)
        places = iota((8, 256), 1)
        rows = iota((8, 256), 0)
        for e in range(LINES):
            line = HALF * LINES + col * LINES + e + rows
            for source in range(ROWS):
                for half in range(2):
                    wide = pieces[half, source, BLOCKS - 1].astype(F32)
                    for i in range(WIDTH // 2):
                        held = jnp.where((places == line + 64 * i) & (rows < LINES), wide, 0.0)
                        factor = jnp.sum(held, axis=1, keepdims=True)
                        factor = jnp.broadcast_to(factor, (8, 128))
                        b = source * WIDTH + half * (WIDTH // 2) + i
                        for t in range(LINES):
                            base = (e * LINES + t) * RING
                            keep_t[base + b : base + b + 1, :] = factor[t : t + 1]
                            if b < 8:
                                base += SIDE
                                keep_t[base + b : base + b + 1, :] = factor[t : t + 1]
        r_sum[...] = jnp.zeros_like(r_sum)

    def prepare_columns():
        for a in range(SLOTS):
            value = cols[a].astype(F32).reshape(WIDTH * 8, 256)
            if a >= LINES:
                value = jnp.where(col < HALF - 1, value, 0.0)
            for h in range(2):
                col_flat[h, a * 64 : a * 64 + WIDTH * 8, :] = value[:, halves[h]]
                col_flat[h, a * 64 + WIDTH * 8 : a * 64 + 64, :] = jnp.zeros((16, 128), F32)
        for a in range(SLOTS):
            line = ctrial[a // LINES, a % LINES]
            expanded = dot(pick_rows(line, first), spread)
            if a >= LINES:
                expanded = jnp.where(col < HALF - 1, expanded, 0.0)
            for h in range(2):

                def band(number):
                    return col_flat[h, pl.ds(a * 64 + number, 8, stride=8), :]

                for pair in range(2):
                    both = jnp.concatenate([band(2 * pair), band(2 * pair + 1)], axis=0)
                    u_col[a * 32 + pair * 16 : a * 32 + pair * 16 + 16, halves[h]] = both.astype(
                        BF16
                    )
                valence = [band(4 + v) for v in range(4)]
                totals = []
                for c in range(4):
                    total = valence[0] * lane(expanded, c)
                    for v in range(1, 4):
                        total += valence[v] * lane(expanded, 4 * v + c)
                    totals.append(total)
                for pair in range(2):
                    both = jnp.concatenate([totals[2 * pair], totals[2 * pair + 1]], axis=0)
                    y_pair[a * 32 + pair * 16 : a * 32 + pair * 16 + 16, halves[h]] = both.astype(
                        BF16
                    )
        c_sum[...] = jnp.zeros_like(c_sum)

    def one_block(q_value):
        start = lax.rem(first + SIDE - q_value, SIDE)
        inside = (first + iota((8, 128), 0) >= q_value) | (col > 0)
        same = (q_value == 0) & (col == 0)

        def rows(table, t, c, h):
            return table[h, pl.ds((t * 4 + c) * RING + start, 8), :]

        backs = []
        for t in range(LINES):
            backs.append([])
            for c in range(4):
                values = [rows(y_row, t, c, h) for h in range(2)]
                backs[t].append([jnp.concatenate([x, x], axis=0).astype(BF16) for x in values])
        for e in range(LINES):
            tiles = []
            for t in range(LINES):
                a = t + e
                factor = keep_t[pl.ds((e * LINES + t) * RING + start, 8), :]
                if e == 0:
                    factor = jnp.where(inside, factor, 0.0)
                for c in range(4):
                    both = []
                    for h in range(2):
                        kept = rows(left_t, t, c, h) * factor
                        both.append(jnp.concatenate([kept, kept], axis=0).astype(BF16))
                    both = jnp.concatenate(both, axis=1)
                    for pair in range(2):
                        base = a * 32 + pair * 16
                        tiles.append(both * u_col[base : base + 16, :])
            mixed = dot(jnp.concatenate(tiles, axis=0), w_buf[e, q_value]).astype(BF16)
            for t in range(LINES):
                a = t + e
                for h in range(2):
                    products = [[], []]
                    for c in range(4):
                        parts = []
                        for pair in range(2):
                            base = t * 128 + c * 32 + pair * 16
                            piece = mixed[base : base + 16, halves[h]]
                            base = a * 32 + pair * 16
                            parts.append(piece * y_pair[base : base + 16, halves[h]])
                            products[pair].append(piece * backs[t][c][h])
                        total = (parts[0] + parts[1]).astype(F32)
                        r_sum[h, pl.ds((t * 4 + c) * RING + start, 8), :] += total[0:8] + total[8:16]
                    for pair in range(2):
                        some = products[pair]
                        image = ((some[0] + some[1]) + (some[2] + some[3])).astype(F32)
                        if e == 0:
                            image = jnp.where(same, 0.0, image)
                        base = a * 32 + pair * 16
                        c_sum[h, base : base + 16, :] += image

    def finish_rows():
        lanes = iota((SIDE, 128), 1)
        image = jnp.zeros((SIDE, 128), F32)
        for t in range(LINES):
            for c in range(4):
                base = (t * 4 + c) * RING
                total = []
                for h in range(2):
                    head = r_sum[h, base : base + 8, :] + r_sum[h, base + SIDE : base + RING, :]
                    total.append(
                        jnp.concatenate([head, r_sum[h, base + 8 : base + SIDE, :]], axis=0)
                    )
                for v in range(4):
                    product = 0.0
                    for h in range(2):
                        strided = pl.ds(t * 8 * SIDE + 4 + v, SIDE, stride=8)
                        product += flat[h, strided, :] * total[h]
                    value = jnp.sum(product, axis=1, keepdims=True)
                    image = jnp.where(lanes == t * 16 + 4 * v + c, value, image)
        for target in range(ROWS):
            zrow[target, 0:WIDTH, :] = -image[target * WIDTH : (target + 1) * WIDTH]
            zrow[target, WIDTH:8, :] = jnp.zeros((8 - WIDTH, 128), F32)

    def finish_columns():
        lanes = iota((8, 128), 1)
        for a in range(SLOTS):
            image = jnp.zeros((8, 128), F32)
            for v in range(4):
                for c in range(4):
                    product = 0.0
                    for h in range(2):
                        base = (a * 4 + c) * 8
                        strided = pl.ds(a * 64 + 4 + v, 8, stride=8)
                        product += col_flat[h, strided, :] * c_sum[h, base : base + 8, :]
                    value = jnp.sum(product, axis=1, keepdims=True)
                    image = jnp.where(lanes == 4 * v + c, value, image)
            zcol[a] = -image

    def exchange():
        tile = ones_where(iota((16, SIDE * 16), 1) % 16 == iota((16, SIDE * 16), 0))
        own_point = iota((SIDE, SIDE * 16), 1) // 16 == iota((SIDE, SIDE * 16), 0)
        ones = jnp.ones((8, SIDE), BF16)
        points = iota((8, SIDE * 16), 1) // 16
        row_points = first + iota((8, SIDE * 16), 0)
        places = iota((WIDTH, SIDE), 1)
        wide = jnp.concatenate([rvec[t] for t in range(LINES)], axis=0)
        high = wide.astype(BF16)
        low = (wide - high.astype(F32)).astype(BF16)
        split = jnp.concatenate([high, low], axis=0)
        zex[...] = jnp.zeros_like(zex)
        sums = jnp.zeros((8 * LINES, 256), F32)
        for a in range(LINES):
            line = col * LINES + a
            transposed = jnp.transpose(trial_v[a].astype(F32)).astype(BF16)
            values = jnp.where(own_point, dot(transposed, tile), 0.0).astype(BF16)
            values = dot(ones, values)
            kept_values = []
            strict_factors = []
            for t in range(LINES):
                row_line = HALF * LINES + t
                held = jnp.where(places == line, window[t], 0).astype(F32)
                held = jnp.sum(held, axis=1, keepdims=True)
                held = jnp.concatenate([held, jnp.zeros((8 - WIDTH, 1), F32)], axis=0)
                kept = (line > row_line) | ((line == row_line) & (points >= row_points))
                strict = (line > row_line) | ((line == row_line) & (points > row_points))
                kept_values.append(jnp.where(kept, held, 0.0) * values)
                strict_factors.append(jnp.where(strict, held, 0.0))
            table = dens[a].reshape(SIDE * 16, 256)
            sums += dot(jnp.concatenate(kept_values, axis=0).astype(BF16), table)
            products = dot(split, table, (1, 1))
            products = products[0 : 8 * LINES] + products[8 * LINES : 16 * LINES]
            image = jnp.sum(
                products * jnp.concatenate(strict_factors, axis=0), axis=0, keepdims=True
            )
            for target in range(ROWS):
                lanes = slice(target * WIDTH * 16, (target + 1) * WIDTH * 16)
                zex[target, a : a + 1, 0 : WIDTH * 16] = 2.0 * image[:, lanes]
        for t in range(LINES):
            pvec[t] = sums[t * 8 : t * 8 + 8]

    def row_vectors():
        for t in range(LINES):
            diagonal = block_diagonal(trial_v[t], first, WIDTH).astype(BF16)
            scaled = (dens[t, pl.ds(first, WIDTH)].astype(F32) * coulomb[...]).astype(BF16)
            rsend[t] = dot(diagonal, scaled.reshape(WIDTH * 16, 256))

    def exchange_rows():
        total = jnp.zeros((8, 128), F32)
        lanes = WIDTH * 16
        own = iota((8, lanes), 1) // 16 == iota((8, lanes), 0)
        for t in range(LINES):
            summed = pvec[t]
            for j in range(1, HALF):
                summed += pbuf[j, t]
            scaled = (dens[t, pl.ds(first, WIDTH)].astype(F32) * coulomb[...]).astype(BF16)
            scaled = scaled.reshape(lanes, 256)
            high = summed.astype(BF16)
            low = (summed - high.astype(F32)).astype(BF16)
            products = dot(jnp.concatenate([high, low], axis=0), scaled, (1, 1))
            products = jnp.where(own, products[0:8] + products[8:16], 0.0)
            fold = ones_where(iota((lanes, 128), 0) % 16 + t * 16 == iota((lanes, 128), 1), F32)
            total += dot(products, fold, precision=HIGHEST)
        ssum[...] = 2.0 * total

    def final_copies():
        copies = []
        for step in (8, 9, 10, 11, 7, 6, 5, 4, 12, 13, 14, 15, 3, 2, 1):
            peer = lax.rem(col + step, 2 * HALF)
            copies.append(to(ssum, fbuf.at[col], S_FINAL, FINAL, (row, peer)))
        return copies

    def panel_copies():
        return [to(stage.at[j % 2], pieces.at[j % 2, row], S_PANEL, OWN, (row, j)) for j in range(HALF)]

    def trial_copies():
        return [to(trial, ptrial, S_TRIAL + j, PT, (row, j)) for j in range(HALF)]

    def column_copies():
        near = (row, lax.rem(col + HALF, 2 * HALF))
        own = bands.at[:, pl.ds(first, WIDTH)]
        return [
            to(own, cols.at[0:LINES], S_COLUMN, COLS, near),
            to(trial, ctrial.at[0], S_COLUMN + 1, CT, near),
        ]

    def next_copies():
        far = (row, lax.rem(col + HALF - 1, 2 * HALF))
        own = bands.at[0 : LINES - 1, pl.ds(first, WIDTH)]
        return [
            to(own, cols.at[LINES:SLOTS], S_COLUMN + 2, NEXT, far),
            to(trial, ctrial.at[1], S_COLUMN + 3, CTN, far),
        ]

    def vector_copies():
        return [to(rsend, rvec, S_VECTOR + j, RVEC, (row, HALF + j)) for j in range(1, HALF)]

    def piece_copies():
        own = pieces.at[core, row]
        return [
            to(own, own, S_PIECE, PIECE + step, (peer, col)) for step, peer in row_peers()
        ] + [to(own, own, S_TWIN, TWIN, twin)]

    def twin_copies():
        return [
            to(pieces.at[core, source], pieces.at[core, source], S_TWIN, TWIN, twin)
            for step, source in row_sources()
        ]

    def sum_copies():
        return [
            to(zrow.at[peer], rbuf.at[step - 1], S_RSUM, RSUM, (peer, col))
            for step, peer in row_peers()
        ]

    def near_sum():
        return to(zcol.at[0:LINES], cbuf, S_CSUM, CSUM, (row, lax.rem(col + HALF, 2 * HALF)))

    def far_sum():
        return to(
            zcol.at[LINES:SLOTS], dbuf, S_DSUM, DSUM, (row, lax.rem(col + HALF + 1, 2 * HALF))
        )

    def exchange_copies():
        return [
            to(zex.at[peer], ebuf.at[step - 1], S_SWAP, RSUM, (peer, col))
            for step, peer in row_peers()
        ]

    def part_copy():
        return to(pvec, pbuf.at[col - HALF], S_PART, PVEC + col - HALF, (row, HALF))

    greet()

    @pl.when(col < HALF)
    def _():
        for number in range(SIDE // Q_STEP):
            chunk(number).start()

    @pl.when(col == HALF)
    def _():
        for copy in stage_copies():
            copy.start()
        for half in range(2):
            parts = []
            for i in range(WIDTH // 2):
                held = window[:, half * (WIDTH // 2) + i].astype(F32)
                held = jnp.concatenate([held, jnp.zeros((8 - LINES, SIDE), F32)], axis=0)
                parts.append(jnp.concatenate([held, jnp.zeros((8, 64 - SIDE), F32)], axis=1))
            parts.append(jnp.zeros((8, 64), F32))
            stage[half, BLOCKS - 1] = jnp.concatenate(parts, axis=1).astype(BF16)
        for copy in stage_copies():
            copy.wait()

    @pl.when(col >= HALF)
    def _():
        fetch_density().start()

    pl.semaphore_wait(pltpu.get_barrier_semaphore(), ROWS + 2 * HALF - 2)

    @pl.when(col < HALF)
    def _():
        own = pieces.at[core, row]
        to(own, own, 0, OWN, (row, HALF)).wait_recv()
        for copy in piece_copies():
            copy.start()
        for (step, source), forward in zip(row_sources(), twin_copies()):
            piece = pieces.at[core, source]
            to(piece, piece, 0, PIECE + step, (source, col)).wait_recv()
            forward.start()
        to(cols.at[0:LINES], cols.at[0:LINES], 0, COLS, (row, HALF)).wait_recv()
        to(trial, ctrial.at[0], 0, CT, (row, HALF)).wait_recv()

        @pl.when(col < HALF - 1)
        def _():
            to(cols.at[LINES:SLOTS], cols.at[LINES:SLOTS], 0, NEXT, (row, HALF)).wait_recv()
            to(trial, ctrial.at[1], 0, CTN, (row, HALF)).wait_recv()

        prepare_columns()
        for source in range(ROWS):
            unpack_piece(core, source)
        other = pieces.at[1 - core]
        to(other, other, 0, TWIN, twin).wait_recv()
        for source in range(ROWS):
            unpack_piece(1 - core, source)
        to(trial, ptrial, 0, PT, (row, HALF)).wait_recv()
        prepare_panel()
        sent = pieces.at[core, 0 : ROWS - 1]
        to(sent, sent, S_PIECE, 0, twin).wait_send()
        sent = pieces.at[core]
        to(sent, sent, S_TWIN, 0, twin).wait_send()

        def one_chunk(number, carry):
            chunk(number).wait()
            for k in range(Q_STEP):
                one_block(number * Q_STEP + k)
            return carry

        lax.fori_loop(0, SIDE // Q_STEP, one_chunk, 0)
        finish_rows()
        for copy in sum_copies():
            copy.start()
        finish_columns()
        near_sum().start()

        @pl.when(col < HALF - 1)
        def _():
            far_sum().start()

        to(rbuf, rbuf, 0, RSUM, twin).wait_recv()
        total = zrow[row]
        for step in range(ROWS - 1):
            total += rbuf[step]
        ssum[...] = total

    @pl.when(col >= HALF)
    def _():
        @pl.when(col == HALF)
        def _():
            for copy in panel_copies():
                copy.start()

        for copy in column_copies():
            copy.start()

        @pl.when(col > HALF)
        def _():
            for copy in next_copies():
                copy.start()

        fetch_density().wait()

        @pl.when(col == HALF)
        def _():
            for copy in trial_copies():
                copy.start()
            row_vectors()
            for copy in vector_copies():
                copy.start()
            rvec[...] = rsend[...]

        @pl.when(col > HALF)
        def _():
            to(rsend, rvec, 0, RVEC, (row, HALF)).wait_recv()

        exchange()
        for copy in exchange_copies():
            copy.start()

        @pl.when(col > HALF)
        def _():
            part_copy().start()

        @pl.when(col == HALF)
        def _():
            for j in range(1, HALF):
                to(pvec, pbuf.at[j], 0, PVEC + j, (row, HALF)).wait_recv()
            exchange_rows()

    @pl.when(col <= HALF)
    def _():
        for copy in final_copies():
            copy.start()
        fbuf[col] = ssum[...]

    @pl.when(col < HALF)
    def _():
        col_part[...] = jnp.zeros_like(col_part)

    @pl.when(col >= HALF)
    def _():
        to(ebuf, ebuf, 0, RSUM, (row, HALF)).wait_recv()
        swapped = zex[row]
        for step in range(ROWS - 1):
            swapped += ebuf[step]
        for copy in column_copies():
            copy.wait_send()
        to(ebuf, ebuf, S_SWAP, 0, twin).wait_send()

        @pl.when(col > HALF)
        def _():
            for copy in next_copies() + [part_copy()]:
                copy.wait_send()

        @pl.when(col == HALF)
        def _():
            to(pieces.at[0], pieces.at[0], S_PANEL, 0, twin).wait_send()
            for copy in trial_copies() + vector_copies():
                copy.wait_send()

        fold = ones_where(iota((128, 128), 0) % 16 == iota((128, 128), 1), F32)
        spots = iota((8, 128), 1) // 16 == iota((8, 128), 0)
        images = []
        for a in range(LINES):
            images.append(dot(jnp.where(spots, swapped[a : a + 1], 0.0), fold, precision=HIGHEST))
        to(zcol.at[0:LINES], cbuf, 0, CSUM, (row, HALF)).wait_recv()

        @pl.when(col > HALF)
        def _():
            to(zcol.at[LINES:SLOTS], dbuf, 0, DSUM, (row, HALF)).wait_recv()

        for a in range(LINES):
            image = images[a] + cbuf[a]
            if a < LINES - 1:
                image += jnp.where(col > HALF, dbuf[a], 0.0)
            col_part[a] = image

    @pl.when(col <= HALF)
    def _():
        to(fbuf.at[0:HALF], fbuf.at[0:HALF], 0, FINAL, twin).wait_recv()

    @pl.when(col > HALF)
    def _():
        to(fbuf.at[0 : HALF + 1], fbuf.at[0 : HALF + 1], 0, FINAL, twin).wait_recv()

    total = fbuf[0]
    for source in range(1, HALF + 1):
        total += fbuf[source]
    row_part[...] = total

    @pl.when(col < HALF)
    def _():
        to(rbuf, rbuf, S_RSUM, 0, twin).wait_send()
        near_sum().wait_send()

        @pl.when(col < HALF - 1)
        def _():
            far_sum().wait_send()

    @pl.when(col <= HALF)
    def _():
        sent = fbuf.at[0 : 2 * HALF - 1]
        to(sent, sent, S_FINAL, 0, twin).wait_send()


def place_kernel(row_part, col_part, row_image, col_image):
    choose = ones_where(
        iota((8, 128), 1) == iota((8, 128), 0) * 16 + lax.axis_index("col"), F32
    )
    picked = dot(choose, row_part[...], (1, 1), HIGHEST)
    for t in range(LINES):
        row_image[t] = picked[t : t + 1, 0:WIDTH]
    for a in range(LINES):
        col_image[a] = col_part[a, 0:WIDTH, 0:16]


def local(band_factors, pair_density, screened, coulomb, window_mask, trial_vector):
    trial = trial_vector.transpose(1, 0, 2)
    vmem = pltpu.VMEM
    parts = pl.pallas_call(
        panel_product_kernel,
        name="panel_product",
        out_shape=[
            jax.ShapeDtypeStruct((8, 128), F32),
            jax.ShapeDtypeStruct((LINES, 8, 128), F32),
        ],
        in_specs=[ANY, ANY, ANY, ANY, VMEM, VMEM, VMEM],
        out_specs=[VMEM, VMEM],
        scratch_shapes=[
            vmem((LINES, SIDE, 256, 256), BF16),
            vmem((LINES, SIDE, 16, 256), BF16),
            vmem((2, BLOCKS, 8, 256), BF16),
            vmem((2, ROWS, BLOCKS, 8, 256), BF16),
            vmem((SLOTS, WIDTH, 8, 256), BF16),
            vmem((2, LINES, 16, SIDE), BF16),
            vmem((LINES, 16, SIDE), BF16),
            vmem((LINES, 8, 256), F32),
            vmem((LINES, 8, 256), F32),
            vmem((2, LINES * 8 * SIDE, 128), F32),
            vmem((2, LINES * 4 * RING, 128), F32),
            vmem((2, LINES * 4 * RING, 128), F32),
            vmem((LINES * LINES * RING, 128), F32),
            vmem((2, LINES * 4 * RING, 128), F32),
            vmem((2, SLOTS * 64, 128), F32),
            vmem((SLOTS * 32, 256), BF16),
            vmem((SLOTS * 32, 256), BF16),
            vmem((2, SLOTS * 32, 128), F32),
            vmem((ROWS, 8, 128), F32),
            vmem((SLOTS, 8, 128), F32),
            vmem((LINES, 8, 256), F32),
            vmem((ROWS, 8, 128), F32),
            vmem((ROWS - 1, 8, 128), F32),
            vmem((LINES, 8, 128), F32),
            vmem((SLOTS - LINES, 8, 128), F32),
            vmem((HALF, LINES, 8, 256), F32),
            vmem((ROWS - 1, 8, 128), F32),
            vmem((2 * HALF, 8, 128), F32),
            vmem((8, 128), F32),
            pltpu.SemaphoreType.DMA((29,)),
            pltpu.SemaphoreType.DMA((28,)),
            pltpu.SemaphoreType.DMA((7,)),
            pltpu.SemaphoreType.DMA((SIDE // Q_STEP,)),
        ],
        compiler_params=pltpu.CompilerParams(
            collective_id=0, has_side_effects=True, vmem_limit_bytes=56 * 1024 * 1024
        ),
    )(
        band_factors,
        pair_density,
        screened,
        trial,
        window_mask,
        trial,
        coulomb.reshape(1, 256),
    )
    row_image, col_image = pl.pallas_call(
        place_kernel,
        name="place",
        out_shape=[
            jax.ShapeDtypeStruct((LINES, 1, WIDTH), F32),
            jax.ShapeDtypeStruct((LINES, WIDTH, 16), F32),
        ],
        in_specs=[VMEM, VMEM],
        out_specs=[VMEM, VMEM],
    )(*parts)
    return row_image.transpose(1, 0, 2), col_image.transpose(2, 0, 1)


def solution(mesh):
    placed = (
        P("col", None, None, None),
        P("col", None, None, None),
        P("col", None, None, None),
        P(),
        P(None, "row", None),
        P(None, "col", None),
    )
    return jax.shard_map(
        local,
        mesh=mesh,
        in_specs=placed,
        out_specs=(P("col", None, "row"), P(None, "col", "row")),
        check_vma=False,
    )
```

```python
import functools

import jax
import jax.numpy as jnp
from jax import lax
from jax.experimental import pallas as pl
from jax.experimental.pallas import tpu as pltpu
from jax.sharding import PartitionSpec as P

MESH = pl.DeviceIdType.MESH
F32 = jnp.float32
BF16 = jnp.bfloat16
SIDE = 48
ROWS = 8
WIDTH = 6
LINES = 3
HALF = 8
SLOTS = 2 * LINES - 1
RING = SIDE + 8
BLOCKS = LINES * WIDTH // 2 + 1
Q_STEP = 6
HIGHEST = lax.Precision.HIGHEST
ANY = pl.BlockSpec(memory_space=pl.ANY)
VMEM = pl.BlockSpec(memory_space=pltpu.VMEM)


def iota(shape, axis):
    return lax.broadcasted_iota(jnp.int32, shape, axis)


def dot(a, b, contract=(1, 0), precision=None):
    return lax.dot_general(
        a,
        b,
        (((contract[0],), (contract[1],)), ((), ())),
        preferred_element_type=F32,
        precision=precision,
    )


def ones_where(condition, dtype=BF16):
    return jnp.where(condition, 1.0, 0.0).astype(dtype)


def pick_rows(trial_line, first):
    pick = ones_where(iota((8, SIDE), 1) == first + iota((8, SIDE), 0))
    return dot(pick, trial_line, (1, 1)).astype(BF16)


def block_diagonal(trial_line, first, copies):
    rows = pick_rows(trial_line, first)
    tiled = dot(rows, ones_where(iota((16, copies * 16), 1) % 16 == iota((16, copies * 16), 0)))
    return jnp.where(iota(tiled.shape, 1) // 16 == iota(tiled.shape, 0), tiled, 0.0)


def greet():
    row, col = lax.axis_index("row"), lax.axis_index("col")
    barrier = pltpu.get_barrier_semaphore()
    for step in (5, 3, 7, 1, 4, 2, 6):
        pl.semaphore_signal(
            barrier, inc=1, device_id=(lax.rem(row + step, ROWS), col), device_id_type=MESH
        )
    for step in (8, 9, 10, 11, 7, 6, 5, 4, 12, 13, 14, 15, 3, 2, 1):
        pl.semaphore_signal(
            barrier, inc=1, device_id=(row, lax.rem(col + step, 2 * HALF)), device_id_type=MESH
        )


def remote(source, target, send_sem, recv_sem, device):
    return pltpu.make_async_remote_copy(
        src_ref=source,
        dst_ref=target,
        send_sem=send_sem,
        recv_sem=recv_sem,
        device_id=device,
        device_id_type=MESH,
    )


def panel_product_kernel(
    bands,
    density,
    blocks,
    trial,
    window,
    trial_v,
    coulomb,
    row_part,
    col_part,
    w_buf,
    dens,
    stage,
    pieces,
    cols,
    ctrial,
    ptrial,
    rsend,
    rvec,
    flat,
    left_t,
    y_row,
    keep_t,
    r_sum,
    col_flat,
    u_col,
    y_pair,
    c_sum,
    zrow,
    zcol,
    pvec,
    zex,
    rbuf,
    cbuf,
    dbuf,
    pbuf,
    ebuf,
    fbuf,
    ssum,
    send,
    recv,
    local,
    w_sem,
):
    row, col = lax.axis_index("row"), lax.axis_index("col")
    first = row * WIDTH
    core = lax.rem(col, 2)
    twin = (row, col + 1 - 2 * core)
    halves = (slice(0, 128), slice(128, 256))
    spread = ones_where(iota((16, 2048), 1) // 128 == iota((16, 2048), 0))

    def to(source, target, number, arrives, device):
        return remote(source, target, send.at[number], recv.at[arrives], device)

    def row_peers():
        return [(step, lax.rem(row + step, ROWS)) for step in (5, 3, 7, 1, 4, 2, 6)]

    def row_sources():
        return [(step, lax.rem(row + ROWS - step, ROWS)) for step in (2, 6, 4, 1, 7, 3, 5)]

    COLS, NEXT, CT, CTN, PT, OWN, RVEC, TWIN, PIECE = 0, 1, 2, 3, 4, 5, 6, 7, 8
    RSUM, CSUM, DSUM, FINAL, PVEC = 16, 17, 18, 19, 20
    S_PIECE, S_TWIN, S_RSUM, S_CSUM, S_DSUM, S_FINAL, S_SWAP = 0, 1, 2, 3, 4, 5, 6
    S_PANEL, S_TRIAL, S_VECTOR, S_PART, S_COLUMN = 7, 8, 16, 24, 25

    def lane(expanded, s):
        return expanded[:, s * 128 : (s + 1) * 128]

    def chunk(number):
        return pltpu.make_async_copy(
            blocks.at[:, pl.ds(number * Q_STEP, Q_STEP)],
            w_buf.at[:, pl.ds(number * Q_STEP, Q_STEP)],
            w_sem.at[number],
        )

    def stage_copies():
        copies = []
        for half in range(2):
            for t in range(LINES):
                source = bands.at[t, pl.ds(first + half * (WIDTH // 2), WIDTH // 2)]
                number = half * LINES + t
                place = stage.at[half, pl.ds(t * (WIDTH // 2), WIDTH // 2)]
                copies.append(pltpu.make_async_copy(source, place, local.at[1 + number]))
        return copies

    def fetch_density():
        return pltpu.make_async_copy(density, dens, local.at[0])

    def store_ring(table, h, number, value):
        base = number * RING
        table[h, base : base + SIDE, :] = value
        table[h, base + SIDE : base + RING, :] = value[0:8]

    def unpack_piece(half, source):
        for t in range(LINES):
            lines = slice(t * (WIDTH // 2), (t + 1) * (WIDTH // 2))
            value = pieces[half, source, lines].astype(F32).reshape(WIDTH * 4, 256)
            base = pl.multiple_of((t * SIDE + source * WIDTH + half * (WIDTH // 2)) * 8, 8)
            for h in range(2):
                flat[h, pl.ds(base, WIDTH * 4), :] = value[:, halves[h]]

    def prepare_panel():
        for t in range(LINES):
            line = jnp.transpose(ptrial[t].astype(F32)).astype(BF16)
            expanded = dot(line, spread)
            for h in range(2):

                def band(number):
                    return flat[h, pl.ds(t * 8 * SIDE + number, SIDE, stride=8), :]

                for c in range(4):
                    store_ring(left_t, h, t * 4 + c, band(c))
                valence = [band(4 + v) for v in range(4)]
                for c in range(4):
                    total = valence[0] * lane(expanded, c)
                    for v in range(1, 4):
                        total += valence[v] * lane(expanded, 4 * v + c)
                    store_ring(y_row, h, t * 4 + c, total)
        places = iota((8, 256), 1)
        rows = iota((8, 256), 0)
        for e in range(LINES):
            line = HALF * LINES + col * LINES + e + rows
            for source in range(ROWS):
                for half in range(2):
                    wide = pieces[half, source, BLOCKS - 1].astype(F32)
                    for i in range(WIDTH // 2):
                        held = jnp.where((places == line + 64 * i) & (rows < LINES), wide, 0.0)
                        factor = jnp.sum(held, axis=1, keepdims=True)
                        factor = jnp.broadcast_to(factor, (8, 128))
                        b = source * WIDTH + half * (WIDTH // 2) + i
                        for t in range(LINES):
                            base = (e * LINES + t) * RING
                            keep_t[base + b : base + b + 1, :] = factor[t : t + 1]
                            if b < 8:
                                base += SIDE
                                keep_t[base + b : base + b + 1, :] = factor[t : t + 1]
        r_sum[...] = jnp.zeros_like(r_sum)

    def prepare_columns():
        for a in range(SLOTS):
            value = cols[a].astype(F32).reshape(WIDTH * 8, 256)
            if a >= LINES:
                value = jnp.where(col < HALF - 1, value, 0.0)
            for h in range(2):
                col_flat[h, a * 64 : a * 64 + WIDTH * 8, :] = value[:, halves[h]]
                col_flat[h, a * 64 + WIDTH * 8 : a * 64 + 64, :] = jnp.zeros((16, 128), F32)
        for a in range(SLOTS):
            line = ctrial[a // LINES, a % LINES]
            expanded = dot(pick_rows(line, first), spread)
            if a >= LINES:
                expanded = jnp.where(col < HALF - 1, expanded, 0.0)
            for h in range(2):

                def band(number):
                    return col_flat[h, pl.ds(a * 64 + number, 8, stride=8), :]

                for pair in range(2):
                    both = jnp.concatenate([band(2 * pair), band(2 * pair + 1)], axis=0)
                    u_col[a * 32 + pair * 16 : a * 32 + pair * 16 + 16, halves[h]] = both.astype(
                        BF16
                    )
                valence = [band(4 + v) for v in range(4)]
                totals = []
                for c in range(4):
                    total = valence[0] * lane(expanded, c)
                    for v in range(1, 4):
                        total += valence[v] * lane(expanded, 4 * v + c)
                    totals.append(total)
                for pair in range(2):
                    both = jnp.concatenate([totals[2 * pair], totals[2 * pair + 1]], axis=0)
                    y_pair[a * 32 + pair * 16 : a * 32 + pair * 16 + 16, halves[h]] = both.astype(
                        BF16
                    )
        c_sum[...] = jnp.zeros_like(c_sum)

    def one_block(q_value):
        start = lax.rem(first + SIDE - q_value, SIDE)
        inside = (first + iota((8, 128), 0) >= q_value) | (col > 0)
        same = (q_value == 0) & (col == 0)

        def rows(table, t, c, h):
            return table[h, pl.ds((t * 4 + c) * RING + start, 8), :]

        backs = []
        for t in range(LINES):
            backs.append([])
            for c in range(4):
                values = [rows(y_row, t, c, h) for h in range(2)]
                backs[t].append([jnp.concatenate([x, x], axis=0).astype(BF16) for x in values])
        for e in range(LINES):
            tiles = []
            for t in range(LINES):
                a = t + e
                factor = keep_t[pl.ds((e * LINES + t) * RING + start, 8), :]
                if e == 0:
                    factor = jnp.where(inside, factor, 0.0)
                for c in range(4):
                    both = []
                    for h in range(2):
                        kept = rows(left_t, t, c, h) * factor
                        both.append(jnp.concatenate([kept, kept], axis=0).astype(BF16))
                    both = jnp.concatenate(both, axis=1)
                    for pair in range(2):
                        base = a * 32 + pair * 16
                        tiles.append(both * u_col[base : base + 16, :])
            mixed = dot(jnp.concatenate(tiles, axis=0), w_buf[e, q_value]).astype(BF16)
            for t in range(LINES):
                a = t + e
                for h in range(2):
                    products = [[], []]
                    for c in range(4):
                        parts = []
                        for pair in range(2):
                            base = t * 128 + c * 32 + pair * 16
                            piece = mixed[base : base + 16, halves[h]]
                            base = a * 32 + pair * 16
                            parts.append(piece * y_pair[base : base + 16, halves[h]])
                            products[pair].append(piece * backs[t][c][h])
                        total = (parts[0] + parts[1]).astype(F32)
                        r_sum[h, pl.ds((t * 4 + c) * RING + start, 8), :] += total[0:8] + total[8:16]
                    for pair in range(2):
                        some = products[pair]
                        image = ((some[0] + some[1]) + (some[2] + some[3])).astype(F32)
                        if e == 0:
                            image = jnp.where(same, 0.0, image)
                        base = a * 32 + pair * 16
                        c_sum[h, base : base + 16, :] += image

    def finish_rows():
        lanes = iota((SIDE, 128), 1)
        image = jnp.zeros((SIDE, 128), F32)
        for t in range(LINES):
            for c in range(4):
                base = (t * 4 + c) * RING
                total = []
                for h in range(2):
                    head = r_sum[h, base : base + 8, :] + r_sum[h, base + SIDE : base + RING, :]
                    total.append(
                        jnp.concatenate([head, r_sum[h, base + 8 : base + SIDE, :]], axis=0)
                    )
                for v in range(4):
                    product = 0.0
                    for h in range(2):
                        strided = pl.ds(t * 8 * SIDE + 4 + v, SIDE, stride=8)
                        product += flat[h, strided, :] * total[h]
                    value = jnp.sum(product, axis=1, keepdims=True)
                    image = jnp.where(lanes == t * 16 + 4 * v + c, value, image)
        for target in range(ROWS):
            zrow[target, 0:WIDTH, :] = -image[target * WIDTH : (target + 1) * WIDTH]
            zrow[target, WIDTH:8, :] = jnp.zeros((8 - WIDTH, 128), F32)

    def finish_columns():
        lanes = iota((8, 128), 1)
        for a in range(SLOTS):
            image = jnp.zeros((8, 128), F32)
            for v in range(4):
                for c in range(4):
                    product = 0.0
                    for h in range(2):
                        base = (a * 4 + c) * 8
                        strided = pl.ds(a * 64 + 4 + v, 8, stride=8)
                        product += col_flat[h, strided, :] * c_sum[h, base : base + 8, :]
                    value = jnp.sum(product, axis=1, keepdims=True)
                    image = jnp.where(lanes == 4 * v + c, value, image)
            zcol[a] = -image

    def exchange():
        tile = ones_where(iota((16, SIDE * 16), 1) % 16 == iota((16, SIDE * 16), 0))
        own_point = iota((SIDE, SIDE * 16), 1) // 16 == iota((SIDE, SIDE * 16), 0)
        ones = jnp.ones((8, SIDE), BF16)
        points = iota((8, SIDE * 16), 1) // 16
        row_points = first + iota((8, SIDE * 16), 0)
        places = iota((WIDTH, SIDE), 1)
        wide = jnp.concatenate([rvec[t] for t in range(LINES)], axis=0)
        high = wide.astype(BF16)
        low = (wide - high.astype(F32)).astype(BF16)
        split = jnp.concatenate([high, low], axis=0)
        zex[...] = jnp.zeros_like(zex)
        sums = jnp.zeros((8 * LINES, 256), F32)
        for a in range(LINES):
            line = col * LINES + a
            transposed = jnp.transpose(trial_v[a].astype(F32)).astype(BF16)
            values = jnp.where(own_point, dot(transposed, tile), 0.0).astype(BF16)
            values = dot(ones, values)
            kept_values = []
            strict_factors = []
            for t in range(LINES):
                row_line = HALF * LINES + t
                held = jnp.where(places == line, window[t], 0).astype(F32)
                held = jnp.sum(held, axis=1, keepdims=True)
                held = jnp.concatenate([held, jnp.zeros((8 - WIDTH, 1), F32)], axis=0)
                kept = (line > row_line) | ((line == row_line) & (points >= row_points))
                strict = (line > row_line) | ((line == row_line) & (points > row_points))
                kept_values.append(jnp.where(kept, held, 0.0) * values)
                strict_factors.append(jnp.where(strict, held, 0.0))
            table = dens[a].reshape(SIDE * 16, 256)
            sums += dot(jnp.concatenate(kept_values, axis=0).astype(BF16), table)
            products = dot(split, table, (1, 1))
            products = products[0 : 8 * LINES] + products[8 * LINES : 16 * LINES]
            image = jnp.sum(
                products * jnp.concatenate(strict_factors, axis=0), axis=0, keepdims=True
            )
            for target in range(ROWS):
                lanes = slice(target * WIDTH * 16, (target + 1) * WIDTH * 16)
                zex[target, a : a + 1, 0 : WIDTH * 16] = 2.0 * image[:, lanes]
        for t in range(LINES):
            pvec[t] = sums[t * 8 : t * 8 + 8]

    def row_vectors():
        for t in range(LINES):
            diagonal = block_diagonal(trial_v[t], first, WIDTH).astype(BF16)
            scaled = (dens[t, pl.ds(first, WIDTH)].astype(F32) * coulomb[...]).astype(BF16)
            rsend[t] = dot(diagonal, scaled.reshape(WIDTH * 16, 256))

    def exchange_rows():
        total = jnp.zeros((8, 128), F32)
        lanes = WIDTH * 16
        own = iota((8, lanes), 1) // 16 == iota((8, lanes), 0)
        for t in range(LINES):
            summed = pvec[t]
            for j in range(1, HALF):
                summed += pbuf[j, t]
            scaled = (dens[t, pl.ds(first, WIDTH)].astype(F32) * coulomb[...]).astype(BF16)
            scaled = scaled.reshape(lanes, 256)
            high = summed.astype(BF16)
            low = (summed - high.astype(F32)).astype(BF16)
            products = dot(jnp.concatenate([high, low], axis=0), scaled, (1, 1))
            products = jnp.where(own, products[0:8] + products[8:16], 0.0)
            fold = ones_where(iota((lanes, 128), 0) % 16 + t * 16 == iota((lanes, 128), 1), F32)
            total += dot(products, fold, precision=HIGHEST)
        ssum[...] = 2.0 * total

    def final_copies():
        copies = []
        for step in (8, 9, 10, 11, 7, 6, 5, 4, 12, 13, 14, 15, 3, 2, 1):
            peer = lax.rem(col + step, 2 * HALF)
            copies.append(to(ssum, fbuf.at[col], S_FINAL, FINAL, (row, peer)))
        return copies

    def panel_copies():
        return [to(stage.at[j % 2], pieces.at[j % 2, row], S_PANEL, OWN, (row, j)) for j in range(HALF)]

    def trial_copies():
        return [to(trial, ptrial, S_TRIAL + j, PT, (row, j)) for j in range(HALF)]

    def column_copies():
        near = (row, lax.rem(col + HALF, 2 * HALF))
        own = bands.at[:, pl.ds(first, WIDTH)]
        return [
            to(own, cols.at[0:LINES], S_COLUMN, COLS, near),
            to(trial, ctrial.at[0], S_COLUMN + 1, CT, near),
        ]

    def next_copies():
        far = (row, lax.rem(col + HALF - 1, 2 * HALF))
        own = bands.at[0 : LINES - 1, pl.ds(first, WIDTH)]
        return [
            to(own, cols.at[LINES:SLOTS], S_COLUMN + 2, NEXT, far),
            to(trial, ctrial.at[1], S_COLUMN + 3, CTN, far),
        ]

    def vector_copies():
        return [to(rsend, rvec, S_VECTOR + j, RVEC, (row, HALF + j)) for j in range(1, HALF)]

    def piece_copies():
        own = pieces.at[core, row]
        return [
            to(own, own, S_PIECE, PIECE + step, (peer, col)) for step, peer in row_peers()
        ] + [to(own, own, S_TWIN, TWIN, twin)]

    def twin_copies():
        return [
            to(pieces.at[core, source], pieces.at[core, source], S_TWIN, TWIN, twin)
            for step, source in row_sources()
        ]

    def sum_copies():
        return [
            to(zrow.at[peer], rbuf.at[step - 1], S_RSUM, RSUM, (peer, col))
            for step, peer in row_peers()
        ]

    def near_sum():
        return to(zcol.at[0:LINES], cbuf, S_CSUM, CSUM, (row, lax.rem(col + HALF, 2 * HALF)))

    def far_sum():
        return to(
            zcol.at[LINES:SLOTS], dbuf, S_DSUM, DSUM, (row, lax.rem(col + HALF + 1, 2 * HALF))
        )

    def exchange_copies():
        return [
            to(zex.at[peer], ebuf.at[step - 1], S_SWAP, RSUM, (peer, col))
            for step, peer in row_peers()
        ]

    def part_copy():
        return to(pvec, pbuf.at[col - HALF], S_PART, PVEC + col - HALF, (row, HALF))

    greet()

    @pl.when(col < HALF)
    def _():
        for number in range(SIDE // Q_STEP):
            chunk(number).start()

    @pl.when(col == HALF)
    def _():
        for copy in stage_copies():
            copy.start()
        for half in range(2):
            parts = []
            for i in range(WIDTH // 2):
                held = window[:, half * (WIDTH // 2) + i].astype(F32)
                held = jnp.concatenate([held, jnp.zeros((8 - LINES, SIDE), F32)], axis=0)
                parts.append(jnp.concatenate([held, jnp.zeros((8, 64 - SIDE), F32)], axis=1))
            parts.append(jnp.zeros((8, 64), F32))
            stage[half, BLOCKS - 1] = jnp.concatenate(parts, axis=1).astype(BF16)
        for copy in stage_copies():
            copy.wait()

    @pl.when(col >= HALF)
    def _():
        fetch_density().start()

    pl.semaphore_wait(pltpu.get_barrier_semaphore(), ROWS + 2 * HALF - 2)

    @pl.when(col < HALF)
    def _():
        own = pieces.at[core, row]
        to(own, own, 0, OWN, (row, HALF)).wait_recv()
        for copy in piece_copies():
            copy.start()
        for (step, source), forward in zip(row_sources(), twin_copies()):
            piece = pieces.at[core, source]
            to(piece, piece, 0, PIECE + step, (source, col)).wait_recv()
            forward.start()
        to(cols.at[0:LINES], cols.at[0:LINES], 0, COLS, (row, HALF)).wait_recv()
        to(trial, ctrial.at[0], 0, CT, (row, HALF)).wait_recv()

        @pl.when(col < HALF - 1)
        def _():
            to(cols.at[LINES:SLOTS], cols.at[LINES:SLOTS], 0, NEXT, (row, HALF)).wait_recv()
            to(trial, ctrial.at[1], 0, CTN, (row, HALF)).wait_recv()

        prepare_columns()
        for source in range(ROWS):
            unpack_piece(core, source)
        other = pieces.at[1 - core]
        to(other, other, 0, TWIN, twin).wait_recv()
        for source in range(ROWS):
            unpack_piece(1 - core, source)
        to(trial, ptrial, 0, PT, (row, HALF)).wait_recv()
        prepare_panel()
        sent = pieces.at[core, 0 : ROWS - 1]
        to(sent, sent, S_PIECE, 0, twin).wait_send()
        sent = pieces.at[core]
        to(sent, sent, S_TWIN, 0, twin).wait_send()

        def one_chunk(number, carry):
            chunk(number).wait()
            for k in range(Q_STEP):
                one_block(number * Q_STEP + k)
            return carry

        lax.fori_loop(0, SIDE // Q_STEP, one_chunk, 0)
        finish_rows()
        for copy in sum_copies():
            copy.start()
        finish_columns()
        near_sum().start()

        @pl.when(col < HALF - 1)
        def _():
            far_sum().start()

        to(rbuf, rbuf, 0, RSUM, twin).wait_recv()
        total = zrow[row]
        for step in range(ROWS - 1):
            total += rbuf[step]
        ssum[...] = total

    @pl.when(col >= HALF)
    def _():
        @pl.when(col == HALF)
        def _():
            for copy in panel_copies():
                copy.start()

        for copy in column_copies():
            copy.start()

        @pl.when(col > HALF)
        def _():
            for copy in next_copies():
                copy.start()

        fetch_density().wait()

        @pl.when(col == HALF)
        def _():
            for copy in trial_copies():
                copy.start()
            row_vectors()
            for copy in vector_copies():
                copy.start()
            rvec[...] = rsend[...]

        @pl.when(col > HALF)
        def _():
            to(rsend, rvec, 0, RVEC, (row, HALF)).wait_recv()

        exchange()
        for copy in exchange_copies():
            copy.start()

        @pl.when(col > HALF)
        def _():
            part_copy().start()

        @pl.when(col == HALF)
        def _():
            for j in range(1, HALF):
                to(pvec, pbuf.at[j], 0, PVEC + j, (row, HALF)).wait_recv()
            exchange_rows()

    @pl.when(col <= HALF)
    def _():
        for copy in final_copies():
            copy.start()
        fbuf[col] = ssum[...]

    @pl.when(col < HALF)
    def _():
        col_part[...] = jnp.zeros_like(col_part)

    @pl.when(col >= HALF)
    def _():
        to(ebuf, ebuf, 0, RSUM, (row, HALF)).wait_recv()
        swapped = zex[row]
        for step in range(ROWS - 1):
            swapped += ebuf[step]
        for copy in column_copies():
            copy.wait_send()
        to(ebuf, ebuf, S_SWAP, 0, twin).wait_send()

        @pl.when(col > HALF)
        def _():
            for copy in next_copies() + [part_copy()]:
                copy.wait_send()

        @pl.when(col == HALF)
        def _():
            to(pieces.at[0], pieces.at[0], S_PANEL, 0, twin).wait_send()
            for copy in trial_copies() + vector_copies():
                copy.wait_send()

        fold = ones_where(iota((128, 128), 0) % 16 == iota((128, 128), 1), F32)
        spots = iota((8, 128), 1) // 16 == iota((8, 128), 0)
        images = []
        for a in range(LINES):
            images.append(dot(jnp.where(spots, swapped[a : a + 1], 0.0), fold, precision=HIGHEST))
        to(zcol.at[0:LINES], cbuf, 0, CSUM, (row, HALF)).wait_recv()

        @pl.when(col > HALF)
        def _():
            to(zcol.at[LINES:SLOTS], dbuf, 0, DSUM, (row, HALF)).wait_recv()

        for a in range(LINES):
            image = images[a] + cbuf[a]
            if a < LINES - 1:
                image += jnp.where(col > HALF, dbuf[a], 0.0)
            col_part[a] = image

    @pl.when(col <= HALF)
    def _():
        to(fbuf.at[0:HALF], fbuf.at[0:HALF], 0, FINAL, twin).wait_recv()

    @pl.when(col > HALF)
    def _():
        to(fbuf.at[0 : HALF + 1], fbuf.at[0 : HALF + 1], 0, FINAL, twin).wait_recv()

    total = fbuf[0]
    for source in range(1, HALF + 1):
        total += fbuf[source]
    row_part[...] = total

    @pl.when(col < HALF)
    def _():
        to(rbuf, rbuf, S_RSUM, 0, twin).wait_send()
        near_sum().wait_send()

        @pl.when(col < HALF - 1)
        def _():
            far_sum().wait_send()

    @pl.when(col <= HALF)
    def _():
        sent = fbuf.at[0 : 2 * HALF - 1]
        to(sent, sent, S_FINAL, 0, twin).wait_send()


def place_kernel(row_part, col_part, row_image, col_image):
    choose = ones_where(
        iota((8, 128), 1) == iota((8, 128), 0) * 16 + lax.axis_index("col"), F32
    )
    picked = dot(choose, row_part[...], (1, 1), HIGHEST)
    for t in range(LINES):
        row_image[t] = picked[t : t + 1, 0:WIDTH]
    for a in range(LINES):
        col_image[a] = col_part[a, 0:WIDTH, 0:16]


def local(band_factors, pair_density, screened, coulomb, window_mask, trial_vector):
    trial = trial_vector.transpose(1, 0, 2)
    vmem = pltpu.VMEM
    parts = pl.pallas_call(
        panel_product_kernel,
        name="panel_product",
        out_shape=[
            jax.ShapeDtypeStruct((8, 128), F32),
            jax.ShapeDtypeStruct((LINES, 8, 128), F32),
        ],
        in_specs=[ANY, ANY, ANY, ANY, VMEM, VMEM, VMEM],
        out_specs=[VMEM, VMEM],
        scratch_shapes=[
            vmem((LINES, SIDE, 256, 256), BF16),
            vmem((LINES, SIDE, 16, 256), BF16),
            vmem((2, BLOCKS, 8, 256), BF16),
            vmem((2, ROWS, BLOCKS, 8, 256), BF16),
            vmem((SLOTS, WIDTH, 8, 256), BF16),
            vmem((2, LINES, 16, SIDE), BF16),
            vmem((LINES, 16, SIDE), BF16),
            vmem((LINES, 8, 256), F32),
            vmem((LINES, 8, 256), F32),
            vmem((2, LINES * 8 * SIDE, 128), F32),
            vmem((2, LINES * 4 * RING, 128), F32),
            vmem((2, LINES * 4 * RING, 128), F32),
            vmem((LINES * LINES * RING, 128), F32),
            vmem((2, LINES * 4 * RING, 128), F32),
            vmem((2, SLOTS * 64, 128), F32),
            vmem((SLOTS * 32, 256), BF16),
            vmem((SLOTS * 32, 256), BF16),
            vmem((2, SLOTS * 32, 128), F32),
            vmem((ROWS, 8, 128), F32),
            vmem((SLOTS, 8, 128), F32),
            vmem((LINES, 8, 256), F32),
            vmem((ROWS, 8, 128), F32),
            vmem((ROWS - 1, 8, 128), F32),
            vmem((LINES, 8, 128), F32),
            vmem((SLOTS - LINES, 8, 128), F32),
            vmem((HALF, LINES, 8, 256), F32),
            vmem((ROWS - 1, 8, 128), F32),
            vmem((2 * HALF, 8, 128), F32),
            vmem((8, 128), F32),
            pltpu.SemaphoreType.DMA((29,)),
            pltpu.SemaphoreType.DMA((28,)),
            pltpu.SemaphoreType.DMA((7,)),
            pltpu.SemaphoreType.DMA((SIDE // Q_STEP,)),
        ],
        compiler_params=pltpu.CompilerParams(
            collective_id=0, has_side_effects=True, vmem_limit_bytes=56 * 1024 * 1024
        ),
    )(
        band_factors,
        pair_density,
        screened,
        trial,
        window_mask,
        trial,
        coulomb.reshape(1, 256),
    )
    row_image, col_image = pl.pallas_call(
        place_kernel,
        name="place",
        out_shape=[
            jax.ShapeDtypeStruct((LINES, 1, WIDTH), F32),
            jax.ShapeDtypeStruct((LINES, WIDTH, 16), F32),
        ],
        in_specs=[VMEM, VMEM],
        out_specs=[VMEM, VMEM],
    )(*parts)
    return row_image.transpose(1, 0, 2), col_image.transpose(2, 0, 1)


def solution(mesh):
    placed = (
        P("col", None, None, None),
        P("col", None, None, None),
        P("col", None, None, None),
        P(),
        P(None, "row", None),
        P(None, "col", None),
    )
    return jax.shard_map(
        local,
        mesh=mesh,
        in_specs=placed,
        out_specs=(P("col", None, "row"), P(None, "col", "row")),
        check_vma=False,
    )
```
